512 devices in a mesh: rep: 8 (over z_lo), blk: 64 (over y, z_hi, x, core).
Axes of the slice: x: 4, y: 4, z: 16 (z_hi: 2, z_lo: 8; z = z_hi * 8 + z_lo), core: 2. Of those that a mesh axis runs over, the one named last changes fastest.
Arguments:
- features: bfloat16 [65536, 256], P(('rep', 'blk')), may hold values from -6 to 6
- weight: bfloat16 [256, 256], replicated, may hold values from -0.375 to 0.375
- cotangent: bfloat16 [65536, 256], P(('rep', 'blk')), may hold values from -6 to 6
- tile_row: int32 [8, 64, 8, 4], P('rep', 'blk'), may hold values from 0 to 511, as said below
- tile_col: int32 [8, 64, 8, 4], P('rep', 'blk'), may hold values from 0 to 511, as said below
- tile_count: int32 [8, 64, 8], P('rep', 'blk'), may hold values from 1 to 4, as said below
- tile_vals: bfloat16 [8, 64, 8, 4, 128, 128], P('rep', 'blk'), may hold values from 0 to 0.015625
Outputs:
- activations: bfloat16 [65536, 256], P(('rep', 'blk'))
- weight_grad: float32 [256, 256], replicated
- feature_grad: bfloat16 [65536, 256], P(('rep', 'blk'))
The draws below stay inside these ranges and needn't reach their ends.
Inputs may be any that keep to these rules, and one draw needn't show every extreme that they name: In slot (r, p, t, k) the row block lies in row panel p: p * 8 <= tile_row < (p + 1) * 8. The live slots of one (r, p, t) hold distinct (tile_row, tile_col) pairs. In slot (r, p, t, k) the column block lies in column panel q = (p - 8 * r - t) mod 64: q * 8 <= tile_col < (q + 1) * 8. Slots with k >= tile_count[r, p, t] are unused. `tile_count`: the value 4 occurs in every draw.
All inputs are finite; a program needn't handle non-finite values.
Results may differ from the reference program's by a relative error of at most 0.018.
Values may be sent and summed in bfloat16 or wider, within the bound.
A program may use at most 64 MiB of HBM per device.

```python
import math
import jax
import jax.numpy as jnp
from jax import lax

F = 256
TB = 128
SLAB = 128
REPS = 8
PANELS = 64
STEPS = 8
CB = 8
CAP = 4
NODES = 65536


def tile_layout(key):
    places = CB * CB
    scores = jax.random.randint(jax.random.fold_in(key, 11), (REPS, PANELS, STEPS, places), 0, 1 << 20)
    scores = scores * places + jnp.arange(places, dtype=jnp.int32)
    chosen = jnp.argsort(scores, axis=-1, stable=True)[..., :CAP]
    member = jnp.arange(REPS, dtype=jnp.int32)[:, None, None, None]
    group = jnp.arange(PANELS, dtype=jnp.int32)[None, :, None, None]
    visit = jnp.arange(STEPS, dtype=jnp.int32)[None, None, :, None]
    column_panel = (group - STEPS * member - visit) % PANELS
    return (group * CB + chosen // CB, column_panel * CB + chosen % CB)


def draw_tile_row(key, part):
    return tile_layout(key)[0].astype(jnp.int32)


def draw_tile_col(key, part):
    return tile_layout(key)[1].astype(jnp.int32)


def draw_tile_count(key, part):
    heavy = jax.random.randint(jax.random.fold_in(key, 23), (PANELS,), 0, 8) == 0
    picked = jax.random.randint(jax.random.fold_in(key, 29), (), 0, PANELS)
    heavy = heavy | (jnp.arange(PANELS, dtype=jnp.int32) == picked)
    light = jax.random.randint(jax.random.fold_in(key, 31), (REPS, PANELS, STEPS), 1, max(2, CAP // 2 + 1))
    light = jnp.minimum(light, CAP)
    return jnp.where(heavy[None, :, None], CAP, light).astype(jnp.int32)


def steps_of(stream_key, shape, split, low, high):
    gain, own = 1.0, jax.random.fold_in(stream_key, 6)
    for dim, blocks in split:
        steps = jnp.exp(jax.random.uniform(jax.random.fold_in(own, dim), (blocks,), jnp.float32, low / len(split), high / len(split)))
        gain = gain * jnp.repeat(steps, shape[dim] // blocks).reshape([-1 if axis == dim else 1 for axis in range(len(shape))])
    return gain


def normal_values(key, dims, scale, bound, shards=(), kind=jnp.bfloat16):
    entries = jax.random.normal(key, dims, jnp.float32) * scale
    if len(shards) > 0:
        entries = steps_of(key, dims, shards, -0.22, 0.18) * entries
    return jnp.clip(entries, min=-bound, max=bound).astype(kind)


def setup_inputs(seed: int = 0) -> dict:
    key_list = jax.random.split(jax.random.key(seed), 8)
    return {
        "features": normal_values(key_list[0], (NODES, F), 1.0, 6.0, ((0, 512),)),
        "weight": normal_values(key_list[1], (F, F), F ** -0.5, 0.375),
        "cotangent": normal_values(key_list[2], (NODES, F), 1.0, 6.0, ((0, 512),)),
        "tile_row": draw_tile_row(jax.random.fold_in(key_list[7], 71), 0),
        "tile_col": draw_tile_col(jax.random.fold_in(key_list[7], 71), 0),
        "tile_count": draw_tile_count(jax.random.fold_in(key_list[7], 71), 0),
        "tile_vals": jnp.clip(0.015625 * jax.random.uniform(key_list[6], (REPS, PANELS, STEPS, CAP, TB, TB), jnp.float32) ** steps_of(key_list[6], (REPS, PANELS, STEPS, CAP, TB, TB), ((0, 8), (1, 64)), -0.2, 0.2), 0.0, 0.015625).astype(jnp.bfloat16),
    }


def to_panels(nodes):
    width = nodes.shape[-1]
    return nodes.reshape(REPS, PANELS, SLAB, width).transpose(1, 0, 2, 3).reshape(PANELS * CB, TB, width)

def from_panels(blocks):
    width = blocks.shape[-1]
    return blocks.reshape(PANELS, REPS, SLAB, width).transpose(1, 0, 2, 3).reshape(NODES, width)

def block_product(source, tile_row, tile_col, tile_count, tile_vals, transpose):
    width = source.shape[-1]
    groups = REPS * PANELS
    live = (jnp.arange(CAP, dtype=jnp.int32)[None, None, None, :] < tile_count[..., None]).astype(source.dtype)
    row_ids = tile_row.reshape(groups, STEPS * CAP).astype(jnp.int32)
    col_ids = tile_col.reshape(groups, STEPS * CAP).astype(jnp.int32)
    masks = live.reshape(groups, STEPS * CAP)
    tiles = tile_vals.reshape(groups, STEPS * CAP, TB, TB)

    def visit(total, item):
        rows_here, cols_here, mask_here, tiles_here = item
        matrices = tiles_here.astype(source.dtype)
        if transpose:
            picked = source[rows_here]
            product = jnp.einsum('kji,kjf->kif', matrices, picked)
            total = total.at[cols_here].add(product * mask_here[:, None, None])
        else:
            picked = source[cols_here]
            product = jnp.einsum('kij,kjf->kif', matrices, picked)
            total = total.at[rows_here].add(product * mask_here[:, None, None])
        return (total, None)
    start = jnp.zeros((PANELS * CB, TB, width), source.dtype)
    total, _ = lax.scan(visit, start, (row_ids, col_ids, masks, tiles))
    return total

def reference(features, weight, cotangent, tile_row, tile_col, tile_count, tile_vals):
    source = to_panels(features.astype(jnp.float32))
    aggregated = from_panels(block_product(source, tile_row, tile_col, tile_count, tile_vals, False)).astype(jnp.bfloat16)
    preact = jnp.dot(aggregated, weight, preferred_element_type=jnp.float32)
    activations = jax.nn.silu(preact).astype(jnp.bfloat16)
    sigmoid_part = jax.nn.sigmoid(preact)
    slope_grad = (cotangent.astype(jnp.float32) * sigmoid_part * (1.0 + preact * (1.0 - sigmoid_part))).astype(jnp.bfloat16)
    weight_grad = jnp.dot(aggregated.T, slope_grad, preferred_element_type=jnp.float32) * (1.0 / math.sqrt(NODES))
    back_rows = jnp.dot(slope_grad, weight.T, preferred_element_type=jnp.float32).astype(jnp.bfloat16)
    back_source = to_panels(back_rows.astype(jnp.float32))
    feature_grad = from_panels(block_product(back_source, tile_row, tile_col, tile_count, tile_vals, True)).astype(jnp.bfloat16)
    return (activations, weight_grad, feature_grad)
```

```python
import functools
import math

import jax
import jax.numpy as jnp
from jax import lax
from jax.experimental import pallas as pl
from jax.experimental.pallas import tpu as pltpu
from jax.sharding import PartitionSpec as P

BF16 = jnp.bfloat16
F32 = jnp.float32
MESH = pl.DeviceIdType.MESH


def layer_kernel(
    dims,
    feat_ref,
    weight_ref,
    cot_ref,
    row_ref,
    col_ref,
    count_ref,
    tile_ref,
    act_ref,
    wgrad_ref,
    fgrad_ref,
    zbuf,
    feats,
    lhs,
    rhs,
    acc,
    accb,
    rsin,
    gpanel,
    cbuf,
    sibin,
    xout,
    xin,
    yout,
    zpart,
    zin,
    zout,
    w_own,
    w_full,
    w_sib,
    w_half,
    w_xin,
    w_quart,
    w_yin,
    w_eight,
    w_zin,
    send,
    recv,
):
    R, X, Y, Z, S, K, B, nodes = dims
    r = lax.axis_index("rep")
    p = lax.axis_index("blk")
    c = p % 2
    x = (p // 2) % X
    zh = (p // S) % 2
    y = p // (2 * S)
    s = p % S
    z = zh * R + r

    def at(y_, z_, x_, c_):
        return {"rep": z_ % R, "blk": ((y_ * 2 + z_ // R) * X + x_) * 2 + c_}

    def z_dev(off):
        return at(y, (z + off + Z) % Z, x, c)

    def y_dev(off):
        return at((y + off) % Y, z, x, c)

    def x_dev(off):
        return at(y, z, (x + off) % X, c)

    sib = at(y, z, x, 1 - c)
    used = [0]

    def slots(n):
        used[0] += n
        return used[0] - n

    def copy(src, dst, i, dev):
        return pltpu.make_async_remote_copy(
            src_ref=src,
            dst_ref=dst,
            send_sem=send.at[i],
            recv_sem=recv.at[i],
            device_id=dev,
            device_id_type=MESH,
        )

    def arrived(dst, i):
        copy(dst, dst, i, sib).wait_recv()

    peers = [z_dev(d) for d in range(1, Z)] + [y_dev(d) for d in range(1, Y)]
    peers += [x_dev(d) for d in range(1, X)] + [sib]
    barrier = pltpu.get_barrier_semaphore()
    for dev in peers:
        pl.semaphore_signal(barrier, inc=1, device_id=dev, device_id_type=MESH)
    zbuf[z] = feat_ref[...]
    pl.semaphore_wait(barrier, len(peers))

    sent = []

    def go(cp):
        cp.start()
        sent.append(cp)

    def slot_of(n):
        return (z - (n + 1) // 2 + Z) % Z if n % 2 else (z + n // 2) % Z

    q = slots(Z)
    for n in range(Z):
        slot = slot_of(n)
        if n:
            arrived(zbuf.at[slot], q + n)
        for m in (1, 2) if n == 0 else (n + 2,):
            if m < Z:
                go(copy(zbuf.at[slot], zbuf.at[slot], q + m, z_dev(1 if m % 2 else -1)))

    q = slots(2)
    y_moves = []
    for half in range(2):
        e = (2 * y + half + r - zh + R) % R
        w = e % 2
        to = ((e + w) // 2) % Y
        src = zbuf.at[pl.ds(half * R, R)]
        dst = feats.at[s * (1 - w) + S * w]
        here = to == y

        @pl.when(here)
        def _():
            pltpu.make_async_copy(src, dst, recv.at[q + w]).start()

        @pl.when(jnp.logical_not(here))
        def _():
            copy(src, dst, q + w, at(to, z, x, c)).start()

        y_moves.append((src, dst, q + w, to))
    arrived(feats.at[s], q)
    arrived(feats.at[S], q + 1)
    for src, dst, i, to in y_moves:

        @pl.when(to != y)
        def _():
            copy(src, dst, i, sib).wait_send()

    q = slots(X)
    qs = slots(X)
    go(copy(feats.at[s * (1 - c) + S * c], feats.at[s], qs, sib))
    for d in range(1, X):
        xd = (x + d) % X
        later = (x < xd).astype(jnp.int32)
        go(copy(feats.at[s * later + S * (1 - later)], feats.at[s], q + d, x_dev(d)))
    for d in range(1, X):
        slot = feats.at[2 * ((x - d + X) % X) + c]
        arrived(slot, q + d)
        go(copy(slot, slot, qs + d, sib))
    for d in range(X):
        arrived(feats.at[2 * ((x - d + X) % X) + 1 - c], qs + d)

    acc[...] = jnp.zeros_like(acc)

    def forward_step(t, _):
        panel = (s - t + S) % S
        for k in range(K):
            rhs[k * B : (k + 1) * B, :] = feats[panel, col_ref[t, k] % R]
            row = row_ref[t, k] % R
            live = k < count_ref[t]
            tile = tile_ref[t * K + k]
            for b in range(R):
                keep = jnp.logical_and(live, row == b)
                lhs[b * B : (b + 1) * B, k * B : (k + 1) * B] = jnp.where(
                    keep, tile, jnp.zeros_like(tile)
                )
        for b in range(R):
            rows = slice(b * B, (b + 1) * B)
            acc[rows, :] += jnp.dot(lhs[rows, :], rhs[...], preferred_element_type=F32)
        return 0

    lax.fori_loop(0, S, forward_step, 0)

    q = slots(R)
    for d in range(1, R):
        rd = (r + d) % R
        accb[d] = acc[pl.ds(pl.multiple_of(rd * B, B), B), :].astype(BF16)
        go(copy(accb.at[d], rsin.at[d], q + d, at(y, zh * R + rd, x, c)))
    total = acc[pl.ds(pl.multiple_of(r * B, B), B), :]
    for d in range(1, R):
        arrived(rsin.at[d], q + d)
        total = total + rsin[d].astype(F32)

    agg = total.astype(BF16)
    preact = jnp.dot(agg, weight_ref[...], preferred_element_type=F32)
    sig = 1.0 / (1.0 + jnp.exp(-preact))
    act_ref[...] = (preact * sig).astype(BF16)
    slope = (cot_ref[...].astype(F32) * (sig * (1.0 + preact * (1.0 - sig)))).astype(BF16)
    back = lax.dot_general(
        slope, weight_ref[...], (((1,), (1,)), ((), ())), preferred_element_type=F32
    )
    gpanel[r] = back.astype(BF16)
    q = slots(R)
    for d in range(1, R):
        rd = (r + d) % R
        go(copy(gpanel.at[r], gpanel.at[r], q + d, at(y, zh * R + rd, x, c)))
    w_own[...] = lax.dot_general(
        agg, slope, (((0,), (0,)), ((), ())), preferred_element_type=F32
    )
    half_rows = w_half.shape[0]
    x_rows = w_quart.shape[0]
    y_rows = w_eight.shape[0]

    def w_rows(i, n):
        return pl.ds(pl.multiple_of(i * n, n), n)

    qw = slots(1)
    go(copy(w_own.at[w_rows(1 - c, half_rows)], w_sib, qw, sib))
    for d in range(1, R):
        arrived(gpanel.at[(r - d + R) % R], q + d)
    arrived(w_sib, qw)
    w_half[...] = w_own[w_rows(c, half_rows), :] + w_sib[...]
    qw = slots(X)
    for d in range(1, X):
        xd = (x + d) % X
        go(copy(w_half.at[w_rows(xd, x_rows)], w_xin.at[x], qw + d, x_dev(d)))
    w_xin[x] = w_half[w_rows(x, x_rows), :]

    def backward_step(t, _):
        panel = (s - t + S) % S
        for k in range(K):
            rhs[k * B : (k + 1) * B, :] = gpanel[row_ref[t, k] % R]
            col = col_ref[t, k] % R
            live = k < count_ref[t]
            tile = tile_ref[t * K + k].T
            for b in range(R):
                keep = jnp.logical_and(live, col == b)
                lhs[b * B : (b + 1) * B, k * B : (k + 1) * B] = jnp.where(
                    keep, tile, jnp.zeros_like(tile)
                )
        for b in range(R):
            rows = slice(b * B, (b + 1) * B)
            cbuf[panel, b] = jnp.dot(
                lhs[rows, :], rhs[...], preferred_element_type=F32
            ).astype(BF16)
        return 0

    lax.fori_loop(0, S, backward_step, 0)

    qs = slots(X)
    for d in list(range(1, X)) + [0]:
        go(copy(cbuf.at[2 * ((x + d) % X) + 1 - c], sibin.at[d], qs + d, sib))

    for d in range(1, X):
        arrived(w_xin.at[(x - d + X) % X], qw + d)
    w_quart[...] = functools.reduce(lambda a, b: a + b, [w_xin[i] for i in range(X)])
    qw = slots(Y)
    for d in range(1, Y):
        yd = (y + d) % Y
        go(copy(w_quart.at[w_rows(yd, y_rows)], w_yin.at[y], qw + d, y_dev(d)))
    w_yin[y] = w_quart[w_rows(y, y_rows), :]

    q = slots(X)
    for d in range(1, X):
        arrived(sibin.at[d], qs + d)
        for b in range(R):
            xout[d, b] = (
                cbuf[2 * ((x + d) % X) + c, b].astype(F32) + sibin[d, b].astype(F32)
            ).astype(BF16)
        go(copy(xout.at[d], xin.at[d], q + d, x_dev(d)))

    for d in range(1, Y):
        arrived(w_yin.at[(y - d + Y) % Y], qw + d)
    w_eight[...] = functools.reduce(lambda a, b: a + b, [w_yin[i] for i in range(Y)])
    w_zin[z] = w_eight[...]
    qw = slots(Z)
    for d in range(1, Z):
        go(copy(w_eight, w_zin.at[z], qw + d, z_dev(d)))

    arrived(sibin.at[0], qs)
    for d in range(1, X):
        arrived(xin.at[d], q + d)
    for b in range(R):
        mine = sibin[0, b].astype(F32)
        first = cbuf[s, b].astype(F32) + jnp.where(c == 0, mine, 0.0)
        second = jnp.where(c == 1, mine, 0.0)
        for d in range(1, X):
            part = xin[d, b].astype(F32)
            above = (x - d + X) % X > x
            first = first + jnp.where(above, part, 0.0)
            second = second + jnp.where(above, 0.0, part)
        yout[0, b] = first.astype(BF16)
        yout[1, b] = second.astype(BF16)

    q = slots(2)
    y_moves = []
    for w in range(2):
        panel = (2 * y + zh - r - w + 2 * R) % R
        to, half = panel // 2, panel % 2
        dst = zpart.at[pl.ds(half * R, R)]

        @pl.when(to == y)
        def _():
            pltpu.make_async_copy(yout.at[w], dst, recv.at[q + half]).start()

        @pl.when(to != y)
        def _():
            copy(yout.at[w], dst, q + half, at(to, z, x, c)).start()

        y_moves.append((yout.at[w], dst, q + half, to))

    for d in range(1, Z):
        arrived(w_zin.at[(z - d + Z) % Z], qw + d)
    out_row = c * half_rows + x * x_rows + y * y_rows
    scale = 1.0 / math.sqrt(nodes)
    wgrad_rows = pl.ds(pl.multiple_of(out_row, y_rows), y_rows)
    w_full[wgrad_rows, :] = (
        functools.reduce(lambda a, b: a + b, [w_zin[i] for i in range(Z)]) * scale
    )
    qw = slots(Y)
    for d in range(1, Y):
        go(copy(w_full.at[wgrad_rows], w_full.at[wgrad_rows], qw + d, y_dev(d)))

    for half in range(2):
        arrived(zpart.at[pl.ds(half * R, R)], q + half)

    def w_piece(c_, x_, y_):
        at_row = c_ * half_rows + x_ * x_rows
        if y_ is None:
            return w_full.at[pl.ds(pl.multiple_of(at_row, x_rows), x_rows)]
        at_row = at_row + y_ * y_rows
        return w_full.at[pl.ds(pl.multiple_of(at_row, y_rows), y_rows)]

    for d in range(1, Y):
        arrived(w_piece(c, x, (y - d + Y) % Y), qw + d)
    qw = slots(X)
    piece = w_piece(c, x, None)
    for d in range(1, X):
        go(copy(piece, piece, qw + d, x_dev(d)))

    q = slots(Z)

    def z_step(n):
        slot = slot_of(n)
        src = zpart.at[slot]
        if n + 2 < Z:
            arrived(zin.at[n], q + n)
            zout[n] = (zpart[slot].astype(F32) + zin[n].astype(F32)).astype(BF16)
            src = zout.at[n]
        land = n - 2 if n >= 2 else Z - 1
        go(copy(src, zin.at[land], q + land, z_dev(-1 if n % 2 else 1)))

    for n in range(Z - 1, Z // 2 - 1, -1):
        z_step(n)
    for d in range(1, X):
        arrived(w_piece(c, (x - d + X) % X, None), qw + d)
    qw = slots(1)
    rows = w_full.at[w_rows(c, half_rows)]
    go(copy(rows, rows, qw, sib))
    for n in range(Z // 2 - 1, 0, -1):
        z_step(n)
    arrived(zin.at[Z - 1], q + Z - 1)
    arrived(zin.at[0], q)
    fgrad_ref[...] = (
        zpart[z].astype(F32) + zin[Z - 1].astype(F32) + zin[0].astype(F32)
    ).astype(BF16)
    arrived(w_full.at[w_rows(1 - c, half_rows)], qw)
    wgrad_ref[...] = w_full[...]

    for src, dst, i, to in y_moves:

        @pl.when(to != y)
        def _():
            copy(src, dst, i, sib).wait_send()

    for cp in sent:
        cp.wait_send()


def on_device(features, weight, cotangent, tile_row, tile_col, tile_count, tile_vals):
    B, F = features.shape
    R = lax.axis_size("rep")
    S = lax.axis_size("blk") // R
    K = tile_vals.shape[3]
    X, Y, Z = S // 2, R // 2, 2 * R
    nodes = B * R * R * S
    dims = (R, X, Y, Z, S, K, B, nodes)
    block = (B, F)
    vmem = pltpu.VMEM
    sems = 3 * Z + 2 + 2 + 6 * X + 2 * R + 2 * Y + 8
    scratch = [
        vmem((Z,) + block, BF16),
        vmem((S + 1, R) + block, BF16),
        vmem((R * B, K * B), BF16),
        vmem((K * B, F), BF16),
        vmem((R * B, F), F32),
        vmem((R,) + block, BF16),
        vmem((R,) + block, BF16),
        vmem((R,) + block, BF16),
        vmem((S, R) + block, BF16),
        vmem((X, R) + block, BF16),
        vmem((X, R) + block, BF16),
        vmem((X, R) + block, BF16),
        vmem((2, R) + block, BF16),
        vmem((Z,) + block, BF16),
        vmem((Z,) + block, BF16),
        vmem((Z,) + block, BF16),
        vmem((F, F), F32),
        vmem((F, F), F32),
        vmem((F // 2, F), F32),
        vmem((F // 2, F), F32),
        vmem((X, F // 2 // X, F), F32),
        vmem((F // 2 // X, F), F32),
        vmem((Y, F // 2 // X // Y, F), F32),
        vmem((F // 2 // X // Y, F), F32),
        vmem((Z, F // 2 // X // Y, F), F32),
        pltpu.SemaphoreType.DMA((sems,)),
        pltpu.SemaphoreType.DMA((sems,)),
    ]
    in_vmem = pl.BlockSpec(memory_space=pltpu.VMEM)
    in_smem = pl.BlockSpec(memory_space=pltpu.SMEM)
    return pl.pallas_call(
        functools.partial(layer_kernel, dims),
        out_shape=(
            jax.ShapeDtypeStruct(block, BF16),
            jax.ShapeDtypeStruct((F, F), F32),
            jax.ShapeDtypeStruct(block, BF16),
        ),
        in_specs=[in_vmem, in_vmem, in_vmem, in_smem, in_smem, in_smem, in_vmem],
        out_specs=(in_vmem, in_vmem, in_vmem),
        scratch_shapes=scratch,
        compiler_params=pltpu.CompilerParams(
            collective_id=0, has_side_effects=True, vmem_limit_bytes=48 << 20
        ),
        name="layer",
    )(
        features,
        weight,
        cotangent,
        tile_row[0, 0],
        tile_col[0, 0],
        tile_count[0, 0],
        tile_vals.reshape((S * K, B, B)),
    )


def solution(mesh):
    return jax.shard_map(
        on_device,
        mesh=mesh,
        in_specs=(
            P(("rep", "blk"), None),
            P(),
            P(("rep", "blk"), None),
            P("rep", "blk", None, None),
            P("rep", "blk", None, None),
            P("rep", "blk", None),
            P("rep", "blk", None, None, None, None),
        ),
        out_specs=(P(("rep", "blk"), None), P(), P(("rep", "blk"), None)),
        check_vma=False,
    )
```

```python
import functools
import math

import jax
import jax.numpy as jnp
from jax import lax
from jax.experimental import pallas as pl
from jax.experimental.pallas import tpu as pltpu
from jax.sharding import PartitionSpec as P

BF16 = jnp.bfloat16
F32 = jnp.float32
MESH = pl.DeviceIdType.MESH


def layer_kernel(
    dims,
    feat_hbm,
    weight_hbm,
    cot_hbm,
    row_hbm,
    col_hbm,
    count_hbm,
    tile_hbm,
    act_ref,
    wgrad_ref,
    fgrad_ref,
    zbuf,
    feats,
    lhs,
    rhs,
    acc,
    accb,
    rsin,
    gpanel,
    cbuf,
    sibin,
    xout,
    xin,
    yout,
    zpart,
    zin,
    zout,
    w_own,
    w_full,
    w_sib,
    w_half,
    w_xin,
    w_quart,
    w_yin,
    w_eight,
    w_zin,
    weight_ref,
    cot_ref,
    row_ref,
    col_ref,
    count_ref,
    tile_ref,
    ysum,
    send,
    recv,
    load,
):
    R, X, Y, Z, S, K, B, nodes = dims
    r = lax.axis_index("rep")
    p = lax.axis_index("blk")
    c = p % 2
    x = (p // 2) % X
    zh = (p // S) % 2
    y = p // (2 * S)
    s = p % S
    z = zh * R + r

    def at(y_, z_, x_, c_):
        return {"rep": z_ % R, "blk": ((y_ * 2 + z_ // R) * X + x_) * 2 + c_}

    def z_dev(off):
        return at(y, (z + off + Z) % Z, x, c)

    def y_dev(off):
        return at((y + off) % Y, z, x, c)

    def x_dev(off):
        return at(y, z, (x + off) % X, c)

    sib = at(y, z, x, 1 - c)
    used = [0]

    def slots(n):
        used[0] += n
        return used[0] - n

    def copy(src, dst, i, dev):
        return pltpu.make_async_remote_copy(
            src_ref=src,
            dst_ref=dst,
            send_sem=send.at[i],
            recv_sem=recv.at[i],
            device_id=dev,
            device_id_type=MESH,
        )

    def arrived(dst, i):
        copy(dst, dst, i, sib).wait_recv()

    loads = [
        pltpu.make_async_copy(src, dst, load.at[i])
        for i, (src, dst) in enumerate(
            [
                (feat_hbm, zbuf.at[z]),
                (row_hbm, row_ref),
                (col_hbm, col_ref),
                (count_hbm, count_ref),
                (tile_hbm, tile_ref),
                (weight_hbm, weight_ref),
                (cot_hbm, cot_ref),
            ]
        )
    ]
    for cp in loads:
        cp.start()

    near = sorted({d % Z for d in (1, 2, -1, -2)} - {0})
    peers = [z_dev(d) for d in near] + [y_dev(d) for d in range(1, Y)]
    peers += [x_dev(d) for d in range(1, X)] + [sib]
    barrier = pltpu.get_barrier_semaphore()
    for dev in peers:
        pl.semaphore_signal(barrier, inc=1, device_id=dev, device_id_type=MESH)
    loads[0].wait()
    pl.semaphore_wait(barrier, len(peers))

    sent = []

    def go(cp):
        cp.start()
        sent.append(cp)

    up, down = Z // 2, Z - 1 - Z // 2
    levels = [[(1, 0)]]
    for top in range(2, up + 2, 2):
        level = [(g, m) for m in (top, top - 1) for g in (1, -1)]
        levels.append([(g, m) for g, m in level if m <= (up if g > 0 else down)])
    order = [e for level in levels for e in level]
    number = {e: n for n, e in enumerate(order)}

    def slot_of(e):
        return (z - e[0] * e[1] + Z) % Z

    def children(e):
        g, m = e
        if m % 2:
            return []
        both = [(1, 1), (-1, 1), (1, 2), (-1, 2)] if m == 0 else [(g, m + 1), (g, m + 2)]
        return [k for k in both if k in number]

    def role_of(e):
        return (zh + r + slot_of(e) // R) % 2

    qz, qy, qx, qs = slots(Z), slots(Z), slots(X * R), slots(X)

    def f_gather(e):
        slot = slot_of(e)
        if e[1]:
            arrived(zbuf.at[slot], qz + number[e])
        for k in children(e)[::-1]:
            hop = k[0] * (k[1] - e[1])
            go(copy(zbuf.at[slot], zbuf.at[slot], qz + number[k], z_dev(hop)))

    def f_y_to(e):
        return ((2 * y + slot_of(e) // R + role_of(e) + r - zh + R) % R) // 2

    def f_y_block(e):
        w = role_of(e)
        return feats.at[s * (1 - w) + S * w, slot_of(e) % R]

    def f_y(e):
        slot, to, i = slot_of(e), f_y_to(e), qy + number[e]

        @pl.when(to == y)
        def _():
            pltpu.make_async_copy(zbuf.at[slot], f_y_block(e), recv.at[i]).start()

        @pl.when(to != y)
        def _():
            copy(zbuf.at[slot], f_y_block(e), i, at(to, z, x, c)).start()

    def f_y_sent(e):
        @pl.when(f_y_to(e) != y)
        def _():
            copy(zbuf.at[slot_of(e)], f_y_block(e), qy + number[e], sib).wait_send()

    def f_x(e):
        w, b = role_of(e), slot_of(e) % R
        src = f_y_block(e)
        arrived(src, qy + number[e])
        for d in range(1, X):

            @pl.when((x < (x + d) % X) == (w == 0))
            def _():
                copy(src, feats.at[s, b], qx + d * R + b, x_dev(d)).start()

        @pl.when(w == c)
        def _():
            shared(src, feats.at[s, b], qs, sib).start()

    def f_core(e):
        w, b = role_of(e), slot_of(e) % R
        for d in range(1, X):
            xs = (x - d + X) % X

            @pl.when((xs < x) == (w == 0))
            def _():
                block = feats.at[2 * xs + c, b]
                arrived(block, qx + d * R + b)
                shared(block, block, qs + d, sib).start()

    def shared(src, dst, i, dev):
        return copy(src, dst, i, dev)

    for n in range(len(levels) + 2):
        if n < len(levels):
            for e in levels[n]:
                f_gather(e)
            for e in levels[n]:
                f_y(e)
        if 0 <= n - 1 < len(levels):
            for e in levels[n - 1]:
                f_x(e)
        if 0 <= n - 2:
            for e in levels[n - 2]:
                f_core(e)
    for d in range(X):
        arrived(feats.at[2 * ((x - d + X) % X) + 1 - c], qs + d)
    for d in range(X):
        copy(feats.at[s], feats.at[s], qs + d, sib).wait_send()
    for d in range(1, X):
        for b in range(R):
            copy(feats.at[s, b], feats.at[s, b], qx + d * R + b, sib).wait_send()
    for e in order:
        f_y_sent(e)
    for cp in loads[1:]:
        cp.wait()

    acc[...] = jnp.zeros_like(acc)

    def forward_step(t, _):
        panel = (s - t + S) % S
        for k in range(K):
            rhs[k * B : (k + 1) * B, :] = feats[panel, col_ref[k, t] % R]
            row = row_ref[k, t] % R
            live = k < count_ref[t]
            tile = tile_ref[t * K + k]
            for b in range(R):
                keep = jnp.logical_and(live, row == b)
                lhs[b * B : (b + 1) * B, k * B : (k + 1) * B] = jnp.where(
                    keep, tile, jnp.zeros_like(tile)
                )
        for b in range(R):
            rows = slice(b * B, (b + 1) * B)
            acc[rows, :] += jnp.dot(lhs[rows, :], rhs[...], preferred_element_type=F32)
        return 0

    lax.fori_loop(0, S, forward_step, 0)

    q = slots(R)
    for d in range(1, R):
        rd = (r + d) % R
        accb[d] = acc[pl.ds(pl.multiple_of(rd * B, B), B), :].astype(BF16)
        go(copy(accb.at[d], rsin.at[d], q + d, at(y, zh * R + rd, x, c)))
    total = acc[pl.ds(pl.multiple_of(r * B, B), B), :]
    for d in range(1, R):
        arrived(rsin.at[d], q + d)
        total = total + rsin[d].astype(F32)

    agg = total.astype(BF16)
    preact = jnp.dot(agg, weight_ref[...], preferred_element_type=F32)
    sig = 1.0 / (1.0 + jnp.exp(-preact))
    slope = (cot_ref[...].astype(F32) * (sig * (1.0 + preact * (1.0 - sig)))).astype(BF16)
    back = lax.dot_general(
        slope, weight_ref[...], (((1,), (1,)), ((), ())), preferred_element_type=F32
    )
    gpanel[r] = back.astype(BF16)
    q = slots(R)
    for d in range(1, R):
        rd = (r + d) % R
        go(copy(gpanel.at[r], gpanel.at[r], q + d, at(y, zh * R + rd, x, c)))
    act_ref[...] = (preact * sig).astype(BF16)
    w_own[...] = lax.dot_general(
        agg, slope, (((0,), (0,)), ((), ())), preferred_element_type=F32
    )
    half_rows = w_half.shape[0]
    x_rows = w_quart.shape[0]
    y_rows = w_eight.shape[0]

    def w_rows(i, n):
        return pl.ds(pl.multiple_of(i * n, n), n)

    qw = slots(1)
    go(copy(w_own.at[w_rows(1 - c, half_rows)], w_sib, qw, sib))
    for d in range(1, R):
        arrived(gpanel.at[(r - d + R) % R], q + d)
    arrived(w_sib, qw)
    w_half[...] = w_own[w_rows(c, half_rows), :] + w_sib[...]
    qw = slots(X)
    for d in range(1, X):
        xd = (x + d) % X
        go(copy(w_half.at[w_rows(xd, x_rows)], w_xin.at[x], qw + d, x_dev(d)))
    w_xin[x] = w_half[w_rows(x, x_rows), :]

    def backward_step(t, _):
        panel = (s - t + S) % S
        for k in range(K):
            rhs[k * B : (k + 1) * B, :] = gpanel[row_ref[k, t] % R]
            col = col_ref[k, t] % R
            live = k < count_ref[t]
            tile = tile_ref[t * K + k].T
            for b in range(R):
                keep = jnp.logical_and(live, col == b)
                lhs[b * B : (b + 1) * B, k * B : (k + 1) * B] = jnp.where(
                    keep, tile, jnp.zeros_like(tile)
                )
        for b in range(R):
            rows = slice(b * B, (b + 1) * B)
            cbuf[panel, b] = jnp.dot(
                lhs[rows, :], rhs[...], preferred_element_type=F32
            ).astype(BF16)

        @pl.when(panel % 2 != c)
        def _():
            d = (panel // 2 - x + X) % X
            copy(cbuf.at[panel], sibin.at[d], qs + d, sib).start()

        return 0

    qs = slots(X)
    lax.fori_loop(0, S, backward_step, 0)

    qx, qy, qz = slots(X * R), slots(Z), slots(Z)

    def b_x(e):
        w, b = role_of(e), slot_of(e) % R
        for d in range(1, X):
            xd = (x + d) % X

            @pl.when((xd < x) == (w == 0))
            def _():
                xout[d, b] = (
                    cbuf[2 * xd + c, b].astype(F32) + sibin[d, b].astype(F32)
                ).astype(BF16)
                copy(xout.at[d, b], xin.at[d, b], qx + d * R + b, x_dev(d)).start()

    def b_y_to(e):
        return ((2 * y + zh - r - role_of(e) + 2 * R) % R) // 2

    def b_y(e):
        w, b, i = role_of(e), slot_of(e) % R, qy + number[e]
        own = cbuf[s, b].astype(F32)
        other = sibin[0, b].astype(F32)
        ysum[...] = jnp.where(w == 0, own, 0.0) + jnp.where(w == c, other, 0.0)
        for d in range(1, X):

            @pl.when(((x - d + X) % X > x) == (w == 0))
            def _():
                arrived(xin.at[d, b], qx + d * R + b)
                ysum[...] += xin[d, b].astype(F32)

        src = yout.at[number[e]]
        src[...] = ysum[...].astype(BF16)
        dst, to = zpart.at[slot_of(e)], b_y_to(e)

        @pl.when(to == y)
        def _():
            pltpu.make_async_copy(src, dst, recv.at[i]).start()

        @pl.when(to != y)
        def _():
            copy(src, dst, i, at(to, z, x, c)).start()

    def b_y_sent(e):
        @pl.when(b_y_to(e) != y)
        def _():
            copy(yout.at[0], yout.at[0], qy + number[e], sib).wait_send()

    def b_z(e):
        g, m = e
        slot, n = slot_of(e), number[e]
        arrived(zpart.at[slot], qy + n)
        val = zpart[slot].astype(F32)
        for k in children(e):
            arrived(zin.at[number[k]], qz + number[k])
            val = val + zin[number[k]].astype(F32)
        if m == 0:
            fgrad_ref[...] = val.astype(BF16)
        else:
            zout[n] = val.astype(BF16)
            go(copy(zout.at[n], zin.at[n], qz + n, z_dev(-g * (2 - m % 2))))

    def w_piece(c_, x_, y_):
        at_row = c_ * half_rows + x_ * x_rows
        if y_ is None:
            return w_full.at[pl.ds(pl.multiple_of(at_row, x_rows), x_rows)]
        at_row = at_row + y_ * y_rows
        return w_full.at[pl.ds(pl.multiple_of(at_row, y_rows), y_rows)]

    def w_1():
        for d in range(1, X):
            arrived(w_xin.at[(x - d + X) % X], qw + d)
        w_quart[...] = functools.reduce(lambda a, b: a + b, [w_xin[i] for i in range(X)])
        i = slots(Y)
        for d in range(1, Y):
            yd = (y + d) % Y
            go(copy(w_quart.at[w_rows(yd, y_rows)], w_yin.at[y], i + d, y_dev(d)))
        w_yin[y] = w_quart[w_rows(y, y_rows), :]
        return i

    def w_2(i):
        for d in range(1, Y):
            arrived(w_yin.at[(y - d + Y) % Y], i + d)
        w_eight[...] = functools.reduce(lambda a, b: a + b, [w_yin[i] for i in range(Y)])
        w_zin[z] = w_eight[...]
        i = slots(Z)
        for d in range(1, Z):
            go(copy(w_eight, w_zin.at[z], i + d, z_dev(d)))
        return i

    def w_3(i):
        for d in range(1, Z):
            arrived(w_zin.at[(z - d + Z) % Z], i + d)
        piece = w_piece(c, x, y)
        piece[...] = functools.reduce(
            lambda a, b: a + b, [w_zin[i] for i in range(Z)]
        ) * (1.0 / math.sqrt(nodes))
        i = slots(Y)
        for d in range(1, Y):
            go(copy(piece, piece, i + d, y_dev(d)))
        return i

    def w_4(i):
        for d in range(1, Y):
            arrived(w_piece(c, x, (y - d + Y) % Y), i + d)
        piece = w_piece(c, x, None)
        i = slots(X)
        for d in range(1, X):
            go(copy(piece, piece, i + d, x_dev(d)))
        return i

    def w_5(i):
        for d in range(1, X):
            arrived(w_piece(c, (x - d + X) % X, None), i + d)
        rows = w_full.at[w_rows(c, half_rows)]
        i = slots(1)
        go(copy(rows, rows, i, sib))
        return i

    for d in range(X):
        arrived(sibin.at[d], qs + d)
    back_levels = levels[::-1]
    w_state = w_1()
    w_rest = [w_2, w_3, w_4, w_5]
    for n in range(len(levels) + 2):
        if n < len(levels):
            for e in back_levels[n]:
                b_x(e)
        if 0 <= n - 1 < len(levels):
            for e in back_levels[n - 1]:
                b_y(e)
        if 0 <= n - 2:
            for e in back_levels[n - 2]:
                b_z(e)
        if n >= 1 and w_rest:
            w_state = w_rest.pop(0)(w_state)
    while w_rest:
        w_state = w_rest.pop(0)(w_state)
    arrived(w_full.at[w_rows(1 - c, half_rows)], w_state)
    wgrad_ref[...] = w_full[...]

    for d in range(X):
        copy(cbuf.at[0], cbuf.at[0], qs + d, sib).wait_send()
    for d in range(1, X):
        for b in range(R):
            copy(xout.at[d, b], xout.at[d, b], qx + d * R + b, sib).wait_send()
    for e in order:
        b_y_sent(e)
    for cp in sent:
        cp.wait_send()


def on_device(features, weight, cotangent, tile_row, tile_col, tile_count, tile_vals):
    B, F = features.shape
    R = lax.axis_size("rep")
    S = lax.axis_size("blk") // R
    K = tile_vals.shape[3]
    X, Y, Z = S // 2, R // 2, 2 * R
    nodes = B * R * R * S
    dims = (R, X, Y, Z, S, K, B, nodes)
    block = (B, F)
    vmem = pltpu.VMEM
    sems = 5 * Z + 2 * X * R + 4 * X + 2 * R + 2 * Y + 8
    scratch = [
        vmem((Z,) + block, BF16),
        vmem((S + 1, R) + block, BF16),
        vmem((R * B, K * B), BF16),
        vmem((K * B, F), BF16),
        vmem((R * B, F), F32),
        vmem((R,) + block, BF16),
        vmem((R,) + block, BF16),
        vmem((R,) + block, BF16),
        vmem((S, R) + block, BF16),
        vmem((X, R) + block, BF16),
        vmem((X, R) + block, BF16),
        vmem((X, R) + block, BF16),
        vmem((Z,) + block, BF16),
        vmem((Z,) + block, BF16),
        vmem((Z,) + block, BF16),
        vmem((Z,) + block, BF16),
        vmem((F, F), F32),
        vmem((F, F), F32),
        vmem((F // 2, F), F32),
        vmem((F // 2, F), F32),
        vmem((X, F // 2 // X, F), F32),
        vmem((F // 2 // X, F), F32),
        vmem((Y, F // 2 // X // Y, F), F32),
        vmem((F // 2 // X // Y, F), F32),
        vmem((Z, F // 2 // X // Y, F), F32),
        vmem((F, F), BF16),
        vmem(block, BF16),
        pltpu.SMEM((K, S), jnp.int32),
        pltpu.SMEM((K, S), jnp.int32),
        pltpu.SMEM((S,), jnp.int32),
        vmem((S * K, B, B), BF16),
        vmem(block, F32),
        pltpu.SemaphoreType.DMA((sems,)),
        pltpu.SemaphoreType.DMA((sems,)),
        pltpu.SemaphoreType.DMA((7,)),
    ]
    in_vmem = pl.BlockSpec(memory_space=pltpu.VMEM)
    in_hbm = pl.BlockSpec(memory_space=pltpu.HBM)
    return pl.pallas_call(
        functools.partial(layer_kernel, dims),
        out_shape=(
            jax.ShapeDtypeStruct(block, BF16),
            jax.ShapeDtypeStruct((F, F), F32),
            jax.ShapeDtypeStruct(block, BF16),
        ),
        in_specs=[in_hbm] * 7,
        out_specs=(in_vmem, in_vmem, in_vmem),
        scratch_shapes=scratch,
        compiler_params=pltpu.CompilerParams(
            collective_id=0, has_side_effects=True, vmem_limit_bytes=63 << 20
        ),
        name="layer",
    )(
        features,
        weight,
        cotangent,
        tile_row[0, 0].T,
        tile_col[0, 0].T,
        tile_count[0, 0],
        tile_vals.reshape((S * K, B, B)),
    )


def solution(mesh):
    return jax.shard_map(
        on_device,
        mesh=mesh,
        in_specs=(
            P(("rep", "blk"), None),
            P(),
            P(("rep", "blk"), None),
            P("rep", "blk", None, None),
            P("rep", "blk", None, None),
            P("rep", "blk", None),
            P("rep", "blk", None, None, None, None),
        ),
        out_specs=(P(("rep", "blk"), None), P(), P(("rep", "blk"), None)),
        check_vma=False,
    )
```

```python
import functools
import math

import jax
import jax.numpy as jnp
from jax import lax
from jax.experimental import pallas as pl
from jax.experimental.pallas import tpu as pltpu
from jax.sharding import PartitionSpec as P

BF16 = jnp.bfloat16
LATE = 2.5
BLATE = 2.5
F32 = jnp.float32
MESH = pl.DeviceIdType.MESH


def layer_kernel(
    dims,
    feat_hbm,
    weight_hbm,
    cot_hbm,
    row_hbm,
    col_hbm,
    count_hbm,
    tile_hbm,
    act_ref,
    wgrad_ref,
    fgrad_ref,
    zbuf,
    feats_0,
    feats_1,
    lhs,
    rhs,
    acc,
    accb,
    rsin,
    rsown,
    agg_ref,
    gpanel_0,
    gpanel_1,
    cbuf,
    sibin,
    xout,
    xin,
    yout,
    zpart,
    zin,
    zout,
    w_own,
    w_full,
    w_sib,
    w_half,
    w_xin,
    w_quart,
    w_yin,
    w_eight,
    w_zin,
    weight_ref,
    cot_ref,
    row_ref,
    col_ref,
    count_ref,
    tile_ref,
    ysum,
    send,
    recv,
    load,
):
    R, X, Y, Z, S, K, B, HF, nodes = dims
    feats, gpanel = (feats_0, feats_1), (gpanel_0, gpanel_1)
    r = lax.axis_index("rep")
    p = lax.axis_index("blk")
    c = p % 2
    x = (p // 2) % X
    zh = (p // S) % 2
    y = p // (2 * S)
    s = p % S
    z = zh * R + r

    def at(y_, z_, x_, c_):
        return {"rep": z_ % R, "blk": ((y_ * 2 + z_ // R) * X + x_) * 2 + c_}

    def z_dev(off):
        return at(y, (z + off + Z) % Z, x, c)

    def y_dev(off):
        return at((y + off) % Y, z, x, c)

    def x_dev(off):
        return at(y, z, (x + off) % X, c)

    sib = at(y, z, x, 1 - c)
    used = [0]

    def slots(n):
        used[0] += n
        return used[0] - n

    def copy(src, dst, i, dev):
        return pltpu.make_async_remote_copy(
            src_ref=src,
            dst_ref=dst,
            send_sem=send.at[i],
            recv_sem=recv.at[i],
            device_id=dev,
            device_id_type=MESH,
        )

    def arrived(dst, i):
        copy(dst, dst, i, sib).wait_recv()

    def half_cols(h):
        return pl.ds(h * HF, HF)

    loads = [
        pltpu.make_async_copy(src, dst, load.at[i])
        for i, (src, dst) in enumerate(
            [
                (feat_hbm.at[:, half_cols(0)], zbuf.at[0, z]),
                (feat_hbm.at[:, half_cols(1)], zbuf.at[1, z]),
                (row_hbm, row_ref),
                (col_hbm, col_ref),
                (count_hbm, count_ref),
                (tile_hbm, tile_ref),
                (weight_hbm, weight_ref),
                (cot_hbm, cot_ref),
            ]
        )
    ]
    for cp in loads:
        cp.start()

    near = sorted({d % Z for d in (1, 2, -1, -2)} - {0})
    peers = [z_dev(d) for d in near] + [y_dev(d) for d in range(1, Y)]
    peers += [x_dev(d) for d in range(1, X)] + [sib]
    barrier = pltpu.get_barrier_semaphore()
    for dev in peers:
        pl.semaphore_signal(barrier, inc=1, device_id=dev, device_id_type=MESH)
    loads[0].wait()
    loads[1].wait()
    pl.semaphore_wait(barrier, len(peers))

    sent = []

    def go(cp):
        cp.start()
        sent.append(cp)

    up, down = Z // 2, Z - 1 - Z // 2
    levels = [[(1, 0)]]
    for top in range(2, up + 2, 2):
        level = [(g, m) for m in (top, top - 1) for g in (1, -1)]
        levels.append([(g, m) for g, m in level if m <= (up if g > 0 else down)])
    order = [e for level in levels for e in level]
    number = {e: n for n, e in enumerate(order)}

    def slot_of(e):
        return (z - e[0] * e[1] + Z) % Z

    def children(e):
        g, m = e
        if m % 2:
            return []
        both = [(1, 1), (-1, 1), (1, 2), (-1, 2)] if m == 0 else [(g, m + 1), (g, m + 2)]
        return [k for k in both if k in number]

    def role_of(e):
        return (zh + r + slot_of(e) // R) % 2

    fq = [(slots(Z), slots(Z), slots(X * R), slots(X)) for _ in range(2)]

    def f_gather(h, e):
        slot, qz = slot_of(e), fq[h][0]
        block = zbuf.at[h, slot]
        if e[1]:
            arrived(block, qz + number[e])
        for k in children(e)[::-1]:
            hop = k[0] * (k[1] - e[1])
            go(copy(block, block, qz + number[k], z_dev(hop)))

    def f_y_to(e):
        return ((2 * y + slot_of(e) // R + role_of(e) + r - zh + R) % R) // 2

    def f_y_block(h, e):
        w = role_of(e)
        return feats[h].at[s * (1 - w) + S * w, slot_of(e) % R]

    def f_y(h, e):
        slot, to, i = slot_of(e), f_y_to(e), fq[h][1] + number[e]

        @pl.when(to == y)
        def _():
            pltpu.make_async_copy(
                zbuf.at[h, slot], f_y_block(h, e), recv.at[i]
            ).start()

        @pl.when(to != y)
        def _():
            copy(zbuf.at[h, slot], f_y_block(h, e), i, at(to, z, x, c)).start()

    def f_y_sent(h, e):
        @pl.when(f_y_to(e) != y)
        def _():
            copy(zbuf.at[h, 0], zbuf.at[h, 0], fq[h][1] + number[e], sib).wait_send()

    def f_x(h, e):
        w, b = role_of(e), slot_of(e) % R
        src = f_y_block(h, e)
        _, qy, qx, qs = fq[h]
        arrived(src, qy + number[e])
        for d in range(1, X):

            @pl.when((x < (x + d) % X) == (w == 0))
            def _():
                copy(src, feats[h].at[s, b], qx + d * R + b, x_dev(d)).start()

        @pl.when(w == c)
        def _():
            copy(src, feats[h].at[s, b], qs, sib).start()

    def f_core(h, e):
        w, b = role_of(e), slot_of(e) % R
        _, _, qx, qs = fq[h]
        for d in range(1, X):
            xs = (x - d + X) % X

            @pl.when((xs < x) == (w == 0))
            def _():
                block = feats[h].at[2 * xs + c, b]
                arrived(block, qx + d * R + b)
                copy(block, block, qs + d, sib).start()

    def masked_tiles(ids, turned):
        def step(t, _):
            for k in range(K):
                live = k < count_ref[t]
                block = ids[k, t] % R
                tile = tile_ref[t * K + k]
                if turned:
                    tile = tile.T
                for b in range(R):
                    keep = jnp.logical_and(live, block == b)
                    lhs[t, b * B : (b + 1) * B, k * B : (k + 1) * B] = jnp.where(
                        keep, tile, jnp.zeros_like(tile)
                    )
            return 0

        lax.fori_loop(0, S, step, 0)

    def forward_products(h):
        acc[...] = jnp.zeros_like(acc)

        def step(t, _):
            panel = (s - t + S) % S
            for k in range(K):
                rhs[k * B : (k + 1) * B, :] = feats[h][panel, col_ref[k, t] % R]
            for b in range(R):
                rows = slice(b * B, (b + 1) * B)
                acc[rows, :] += jnp.dot(
                    lhs[t, rows, :], rhs[...], preferred_element_type=F32
                )
            return 0

        lax.fori_loop(0, S, step, 0)

    rq = [slots(R), slots(R)]
    own_rows = pl.ds(pl.multiple_of(r * B, B), B)

    def f_finish(h):
        qs = fq[h][3]
        for d in range(X):
            arrived(feats[h].at[2 * ((x - d + X) % X) + 1 - c], qs + d)
        forward_products(h)
        for d in range(1, R):
            rd = (r + d) % R
            accb[h, d] = acc[pl.ds(pl.multiple_of(rd * B, B), B), :].astype(BF16)
            go(copy(accb.at[h, d], rsin.at[h, d], rq[h] + d, at(y, zh * R + rd, x, c)))
        rsown[h] = acc[own_rows, :]

    def f_sent(h):
        _, _, qx, qs = fq[h]
        for d in range(X):
            copy(feats[h].at[0], feats[h].at[0], qs + d, sib).wait_send()
        for d in range(1, X):
            for b in range(R):
                copy(
                    feats[h].at[0, b], feats[h].at[0, b], qx + d * R + b, sib
                ).wait_send()
        for e in order:
            f_y_sent(h, e)

    events = []
    top = len(levels)
    for h in range(2):
        for n in range(top):
            late = n + LATE * h
            events += [(late, 0, "gather", h, n), (late + 1, 1, "x", h, n)]
            events += [(late + 2, 2, "core", h, n)]
        events += [(top + 1.1 + LATE * h, 3, "finish", h, 0)]
    events += [(2.5, 4, "tiles", 0, 0)]
    for _, _, what, h, n in sorted(events):
        if what == "gather":
            for e in levels[n]:
                f_gather(h, e)
            for e in levels[n]:
                f_y(h, e)
        elif what == "x":
            for e in levels[n]:
                f_x(h, e)
        elif what == "core":
            for e in levels[n]:
                f_core(h, e)
        elif what == "tiles":
            for cp in loads[2:]:
                cp.wait()
            masked_tiles(row_ref, False)
        else:
            f_finish(h)
    for h in range(2):
        total = rsown[h]
        for d in range(1, R):
            arrived(rsin.at[h, d], rq[h] + d)
            total = total + rsin[h, d].astype(F32)
        agg_ref[:, h * HF : (h + 1) * HF] = total.astype(BF16)

    agg = agg_ref[...]
    preact = jnp.dot(agg, weight_ref[...], preferred_element_type=F32)
    sig = 1.0 / (1.0 + jnp.exp(-preact))
    slope = (cot_ref[...].astype(F32) * (sig * (1.0 + preact * (1.0 - sig)))).astype(BF16)
    back = lax.dot_general(
        slope, weight_ref[...], (((1,), (1,)), ((), ())), preferred_element_type=F32
    )
    gq = [slots(R), slots(R)]
    for h in range(2):
        gpanel[h][r] = back[:, h * HF : (h + 1) * HF].astype(BF16)
        for d in range(1, R):
            rd = (r + d) % R
            mine = gpanel[h].at[r]
            go(copy(mine, mine, gq[h] + d, at(y, zh * R + rd, x, c)))
    act_ref[...] = (preact * sig).astype(BF16)
    w_own[...] = lax.dot_general(
        agg, slope, (((0,), (0,)), ((), ())), preferred_element_type=F32
    )
    half_rows = w_half.shape[0]
    x_rows = w_quart.shape[0]
    y_rows = w_eight.shape[0]

    def w_rows(i, n):
        return pl.ds(pl.multiple_of(i * n, n), n)

    qw = slots(1)
    go(copy(w_own.at[w_rows(1 - c, half_rows)], w_sib, qw, sib))
    masked_tiles(col_ref, True)
    arrived(w_sib, qw)
    w_half[...] = w_own[w_rows(c, half_rows), :] + w_sib[...]
    qw = slots(X)
    for d in range(1, X):
        xd = (x + d) % X
        go(copy(w_half.at[w_rows(xd, x_rows)], w_xin.at[x], qw + d, x_dev(d)))
    w_xin[x] = w_half[w_rows(x, x_rows), :]

    bq = [(slots(X), slots(X * R), slots(Z), slots(Z)) for _ in range(2)]

    def backward_products(h):
        for d in range(1, R):
            arrived(gpanel[h].at[(r - d + R) % R], gq[h] + d)

        def step(t, _):
            panel = (s - t + S) % S
            for k in range(K):
                rhs[k * B : (k + 1) * B, :] = gpanel[h][row_ref[k, t] % R]
            for b in range(R):
                rows = slice(b * B, (b + 1) * B)
                cbuf[h, panel, b] = jnp.dot(
                    lhs[t, rows, :], rhs[...], preferred_element_type=F32
                ).astype(BF16)

            @pl.when(panel % 2 != c)
            def _():
                d = (panel // 2 - x + X) % X
                copy(cbuf.at[h, panel], sibin.at[h, d], bq[h][0] + d, sib).start()

            return 0

        lax.fori_loop(0, S, step, 0)

    def b_x(h, e):
        w, b = role_of(e), slot_of(e) % R
        for d in range(1, X):
            xd = (x + d) % X

            @pl.when((xd < x) == (w == 0))
            def _():
                xout[h, d, b] = (
                    cbuf[h, 2 * xd + c, b].astype(F32) + sibin[h, d, b].astype(F32)
                ).astype(BF16)
                i = bq[h][1] + d * R + b
                copy(xout.at[h, d, b], xin.at[h, d, b], i, x_dev(d)).start()

    def b_y_to(e):
        return ((2 * y + zh - r - role_of(e) + 2 * R) % R) // 2

    def b_y(h, e):
        w, b, i = role_of(e), slot_of(e) % R, bq[h][2] + number[e]
        own = cbuf[h, s, b].astype(F32)
        other = sibin[h, 0, b].astype(F32)
        ysum[...] = jnp.where(w == 0, own, 0.0) + jnp.where(w == c, other, 0.0)
        for d in range(1, X):

            @pl.when(((x - d + X) % X > x) == (w == 0))
            def _():
                arrived(xin.at[h, d, b], bq[h][1] + d * R + b)
                ysum[...] += xin[h, d, b].astype(F32)

        src = yout.at[h, number[e]]
        src[...] = ysum[...].astype(BF16)
        dst, to = zpart.at[h, slot_of(e)], b_y_to(e)

        @pl.when(to == y)
        def _():
            pltpu.make_async_copy(src, dst, recv.at[i]).start()

        @pl.when(to != y)
        def _():
            copy(src, dst, i, at(to, z, x, c)).start()

    def b_y_sent(h, e):
        @pl.when(b_y_to(e) != y)
        def _():
            copy(yout.at[h, 0], yout.at[h, 0], bq[h][2] + number[e], sib).wait_send()

    def b_z(h, e):
        g, m = e
        slot, n, qz = slot_of(e), number[e], bq[h][3]
        arrived(zpart.at[h, slot], bq[h][2] + n)
        val = zpart[h, slot].astype(F32)
        for k in children(e):
            arrived(zin.at[h, number[k]], qz + number[k])
            val = val + zin[h, number[k]].astype(F32)
        if m == 0:
            fgrad_ref[:, h * HF : (h + 1) * HF] = val.astype(BF16)
        else:
            zout[h, n] = val.astype(BF16)
            go(copy(zout.at[h, n], zin.at[h, n], qz + n, z_dev(-g * (2 - m % 2))))

    def w_piece(c_, x_, y_):
        at_row = c_ * half_rows + x_ * x_rows
        if y_ is None:
            return w_full.at[pl.ds(pl.multiple_of(at_row, x_rows), x_rows)]
        at_row = at_row + y_ * y_rows
        return w_full.at[pl.ds(pl.multiple_of(at_row, y_rows), y_rows)]

    def w_1():
        for d in range(1, X):
            arrived(w_xin.at[(x - d + X) % X], qw + d)
        w_quart[...] = functools.reduce(lambda a, b: a + b, [w_xin[i] for i in range(X)])
        i = slots(Y)
        for d in range(1, Y):
            yd = (y + d) % Y
            go(copy(w_quart.at[w_rows(yd, y_rows)], w_yin.at[y], i + d, y_dev(d)))
        w_yin[y] = w_quart[w_rows(y, y_rows), :]
        return i

    def w_2(i):
        for d in range(1, Y):
            arrived(w_yin.at[(y - d + Y) % Y], i + d)
        w_eight[...] = functools.reduce(lambda a, b: a + b, [w_yin[i] for i in range(Y)])
        w_zin[z] = w_eight[...]
        i = slots(Z)
        for d in range(1, Z):
            go(copy(w_eight, w_zin.at[z], i + d, z_dev(d)))
        return i

    def w_3(i):
        for d in range(1, Z):
            arrived(w_zin.at[(z - d + Z) % Z], i + d)
        piece = w_piece(c, x, y)
        piece[...] = functools.reduce(
            lambda a, b: a + b, [w_zin[i] for i in range(Z)]
        ) * (1.0 / math.sqrt(nodes))
        i = slots(Y)
        for d in range(1, Y):
            go(copy(piece, piece, i + d, y_dev(d)))
        return i

    def w_4(i):
        for d in range(1, Y):
            arrived(w_piece(c, x, (y - d + Y) % Y), i + d)
        piece = w_piece(c, x, None)
        i = slots(X)
        for d in range(1, X):
            go(copy(piece, piece, i + d, x_dev(d)))
        return i

    def w_5(i):
        for d in range(1, X):
            arrived(w_piece(c, (x - d + X) % X, None), i + d)
        rows = w_full.at[w_rows(c, half_rows)]
        i = slots(1)
        go(copy(rows, rows, i, sib))
        return i

    back_levels = levels[::-1]
    for h in range(2):
        backward_products(h)
        if h == 0:
            w_state = w_1()
        for d in range(X):
            arrived(sibin.at[h, d], bq[h][0] + d)
        for level in back_levels:
            for e in level:
                b_x(h, e)
    events = []
    for h in range(2):
        for n in range(top):
            late = n + BLATE * h
            events += [(late, 0, "y", h, n), (late + 2, 1, "z", h, n)]
    w_rest = [w_2, w_3, w_4, w_5]
    events += [(1.5 + n * 1.5, 2, "w", 0, n) for n in range(len(w_rest))]
    for _, _, what, h, n in sorted(events):
        if what == "w":
            w_state = w_rest[n](w_state)
        else:
            for e in back_levels[n]:
                (b_y if what == "y" else b_z)(h, e)
    arrived(w_full.at[w_rows(1 - c, half_rows)], w_state)
    wgrad_ref[...] = w_full[...]

    for h in range(2):
        f_sent(h)
        qs, qx, _, _ = bq[h]
        for d in range(X):
            copy(cbuf.at[h, 0], cbuf.at[h, 0], qs + d, sib).wait_send()
        for d in range(1, X):
            for b in range(R):
                copy(
                    xout.at[h, d, b], xout.at[h, d, b], qx + d * R + b, sib
                ).wait_send()
        for e in order:
            b_y_sent(h, e)
    for cp in sent:
        cp.wait_send()


def on_device(features, weight, cotangent, tile_row, tile_col, tile_count, tile_vals):
    B, F = features.shape
    R = lax.axis_size("rep")
    S = lax.axis_size("blk") // R
    K = tile_vals.shape[3]
    X, Y, Z = S // 2, R // 2, 2 * R
    nodes = B * R * R * S
    HF = F // 2
    dims = (R, X, Y, Z, S, K, B, HF, nodes)
    block = (B, F)
    part = (B, HF)
    vmem = pltpu.VMEM
    sems = 9 * Z + 4 * X * R + 8 * X + 4 * R + 2 * Y + 8
    scratch = [
        vmem((2, Z) + part, BF16),
        vmem((S + 1, R) + part, BF16),
        vmem((S + 1, R) + part, BF16),
        vmem((S, R * B, K * B), BF16),
        vmem((K * B, HF), BF16),
        vmem((R * B, HF), F32),
        vmem((2, R) + part, BF16),
        vmem((2, R) + part, BF16),
        vmem((2,) + part, F32),
        vmem(block, BF16),
        vmem((R,) + part, BF16),
        vmem((R,) + part, BF16),
        vmem((2, S, R) + part, BF16),
        vmem((2, X, R) + part, BF16),
        vmem((2, X, R) + part, BF16),
        vmem((2, X, R) + part, BF16),
        vmem((2, Z) + part, BF16),
        vmem((2, Z) + part, BF16),
        vmem((2, Z) + part, BF16),
        vmem((2, Z) + part, BF16),
        vmem((F, F), F32),
        vmem((F, F), F32),
        vmem((F // 2, F), F32),
        vmem((F // 2, F), F32),
        vmem((X, F // 2 // X, F), F32),
        vmem((F // 2 // X, F), F32),
        vmem((Y, F // 2 // X // Y, F), F32),
        vmem((F // 2 // X // Y, F), F32),
        vmem((Z, F // 2 // X // Y, F), F32),
        vmem((F, F), BF16),
        vmem(block, BF16),
        pltpu.SMEM((K, S), jnp.int32),
        pltpu.SMEM((K, S), jnp.int32),
        pltpu.SMEM((S,), jnp.int32),
        vmem((S * K, B, B), BF16),
        vmem(part, F32),
        pltpu.SemaphoreType.DMA((sems,)),
        pltpu.SemaphoreType.DMA((sems,)),
        pltpu.SemaphoreType.DMA((8,)),
    ]
    in_vmem = pl.BlockSpec(memory_space=pltpu.VMEM)
    in_hbm = pl.BlockSpec(memory_space=pltpu.HBM)
    return pl.pallas_call(
        functools.partial(layer_kernel, dims),
        out_shape=(
            jax.ShapeDtypeStruct(block, BF16),
            jax.ShapeDtypeStruct((F, F), F32),
            jax.ShapeDtypeStruct(block, BF16),
        ),
        in_specs=[in_hbm] * 7,
        out_specs=(in_vmem, in_vmem, in_vmem),
        scratch_shapes=scratch,
        compiler_params=pltpu.CompilerParams(
            collective_id=0, has_side_effects=True, vmem_limit_bytes=63 << 20
        ),
        name="layer",
    )(
        features,
        weight,
        cotangent,
        tile_row[0, 0].T,
        tile_col[0, 0].T,
        tile_count[0, 0],
        tile_vals.reshape((S * K, B, B)),
    )


def solution(mesh):
    return jax.shard_map(
        on_device,
        mesh=mesh,
        in_specs=(
            P(("rep", "blk"), None),
            P(),
            P(("rep", "blk"), None),
            P("rep", "blk", None, None),
            P("rep", "blk", None, None),
            P("rep", "blk", None),
            P("rep", "blk", None, None, None, None),
        ),
        out_specs=(P(("rep", "blk"), None), P(), P(("rep", "blk"), None)),
        check_vma=False,
    )
```

```python
import functools
import math

import jax
import jax.numpy as jnp
from jax import lax
from jax.experimental import pallas as pl
from jax.experimental.pallas import tpu as pltpu
from jax.sharding import PartitionSpec as P

BF16 = jnp.bfloat16
LATE = 2.5
BLATE = 2.5
TAIL = True
F32 = jnp.float32
MESH = pl.DeviceIdType.MESH


def layer_kernel(
    dims,
    feat_hbm,
    weight_hbm,
    cot_hbm,
    row_hbm,
    col_hbm,
    count_hbm,
    tile_hbm,
    act_ref,
    wgrad_ref,
    fgrad_ref,
    zbuf,
    feats_0,
    feats_1,
    lhs,
    rhs,
    acc,
    accb,
    rsin,
    rsown,
    agg_ref,
    gpanel_0,
    gpanel_1,
    cbuf,
    sibin,
    xout,
    xin,
    yout,
    zpart,
    zin,
    zout,
    w_own,
    w_full,
    w_sib,
    w_half,
    w_xin,
    w_quart,
    w_yin,
    w_eight,
    w_zin,
    weight_ref,
    cot_ref,
    row_ref,
    col_ref,
    count_ref,
    tile_ref,
    ysum,
    send,
    recv,
    load,
):
    R, X, Y, Z, S, K, B, HF, nodes = dims
    feats, gpanel = (feats_0, feats_1), (gpanel_0, gpanel_1)
    r = lax.axis_index("rep")
    p = lax.axis_index("blk")
    c = p % 2
    x = (p // 2) % X
    zh = (p // S) % 2
    y = p // (2 * S)
    s = p % S
    z = zh * R + r

    def at(y_, z_, x_, c_):
        return {"rep": z_ % R, "blk": ((y_ * 2 + z_ // R) * X + x_) * 2 + c_}

    def z_dev(off):
        return at(y, (z + off + Z) % Z, x, c)

    def y_dev(off):
        return at((y + off) % Y, z, x, c)

    def x_dev(off):
        return at(y, z, (x + off) % X, c)

    sib = at(y, z, x, 1 - c)
    used = [0]

    def slots(n):
        used[0] += n
        return used[0] - n

    def copy(src, dst, i, dev, out=None):
        return pltpu.make_async_remote_copy(
            src_ref=src,
            dst_ref=dst,
            send_sem=send.at[i if out is None else out],
            recv_sem=recv.at[i],
            device_id=dev,
            device_id_type=MESH,
        )

    def left(like, i):
        copy(like, like, i, sib).wait_send()

    def arrived(dst, i):
        copy(dst, dst, i, sib).wait_recv()

    def half_cols(h):
        return pl.ds(h * HF, HF)

    loads = [
        pltpu.make_async_copy(src, dst, load.at[i])
        for i, (src, dst) in enumerate(
            [
                (feat_hbm.at[:, half_cols(0)], zbuf.at[0, z]),
                (feat_hbm.at[:, half_cols(1)], zbuf.at[1, z]),
                (row_hbm, row_ref),
                (col_hbm, col_ref),
                (count_hbm, count_ref),
                (tile_hbm, tile_ref),
                (weight_hbm, weight_ref),
                (cot_hbm, cot_ref),
            ]
        )
    ]
    for cp in loads:
        cp.start()

    near = sorted({d % Z for d in (1, 2, -1, -2)} - {0})
    peers = [z_dev(d) for d in near] + [y_dev(d) for d in range(1, Y)]
    peers += [x_dev(d) for d in range(1, X)] + [sib]
    barrier = pltpu.get_barrier_semaphore()
    for dev in peers:
        pl.semaphore_signal(barrier, inc=1, device_id=dev, device_id_type=MESH)
    loads[0].wait()
    loads[1].wait()
    pl.semaphore_wait(barrier, len(peers))

    sent = []

    def go(cp):
        cp.start()
        sent.append(cp)

    up, down = Z // 2, Z - 1 - Z // 2
    levels = [[(1, 0)]]
    for top in range(2, up + 2, 2):
        level = [(g, m) for m in (top, top - 1) for g in (1, -1)]
        levels.append([(g, m) for g, m in level if m <= (up if g > 0 else down)])
    order = [e for level in levels for e in level]
    number = {e: n for n, e in enumerate(order)}

    def slot_of(e):
        return (z - e[0] * e[1] + Z) % Z

    def children(e):
        g, m = e
        if m % 2:
            return []
        both = [(1, 1), (-1, 1), (1, 2), (-1, 2)] if m == 0 else [(g, m + 1), (g, m + 2)]
        return [k for k in both if k in number]

    def role_of(e):
        return (zh + r + slot_of(e) // R) % 2

    fq = [(slots(Z), slots(Z), slots(X * R), slots(X)) for _ in range(2)]

    def f_gather(h, e):
        slot, qz = slot_of(e), fq[h][0]
        block = zbuf.at[h, slot]
        if e[1]:
            arrived(block, qz + number[e])
        for k in children(e)[::-1]:
            hop = k[0] * (k[1] - e[1])
            copy(block, block, qz + number[k], z_dev(hop), qz).start()

    def f_to(half):
        return ((2 * y + half + (zh + r + half) % 2 + r - zh + R) % R) // 2

    def f_y_to(e):
        return f_to(slot_of(e) // R)

    def f_y_block(h, e):
        w = role_of(e)
        return feats[h].at[s * (1 - w) + S * w, slot_of(e) % R]

    def f_y(h, e):
        slot, to, i = slot_of(e), f_y_to(e), fq[h][1] + number[e]

        @pl.when(to == y)
        def _():
            pltpu.make_async_copy(
                zbuf.at[h, slot], f_y_block(h, e), recv.at[i]
            ).start()

        @pl.when(to != y)
        def _():
            out = fq[h][1] + slot // R
            copy(zbuf.at[h, slot], f_y_block(h, e), i, at(to, z, x, c), out).start()

    def f_x(h, e):
        w, b = role_of(e), slot_of(e) % R
        src = f_y_block(h, e)
        _, qy, qx, qs = fq[h]
        arrived(src, qy + number[e])
        for d in range(1, X):

            @pl.when((x < (x + d) % X) == (w == 0))
            def _():
                i = qx + d * R
                copy(src, feats[h].at[s, b], i + b, x_dev(d), i).start()

        @pl.when(w == c)
        def _():
            copy(src, feats[h].at[s, b], qs, sib).start()

    def f_core(h, e):
        w, b = role_of(e), slot_of(e) % R
        _, _, qx, qs = fq[h]
        for d in range(1, X):
            xs = (x - d + X) % X

            @pl.when((xs < x) == (w == 0))
            def _():
                block = feats[h].at[2 * xs + c, b]
                arrived(block, qx + d * R + b)
                copy(block, block, qs + d, sib).start()

    def masked_tiles(ids, turned):
        def step(t, _):
            for k in range(K):
                live = k < count_ref[t]
                block = ids[k, t] % R
                tile = tile_ref[t * K + k]
                if turned:
                    tile = tile.T
                for b in range(R):
                    keep = jnp.logical_and(live, block == b)
                    lhs[t, b * B : (b + 1) * B, k * B : (k + 1) * B] = jnp.where(
                        keep, tile, jnp.zeros_like(tile)
                    )
            return 0

        lax.fori_loop(0, S, step, 0)

    def forward_products(h):
        acc[...] = jnp.zeros_like(acc)

        def step(t, _):
            panel = (s - t + S) % S
            for k in range(K):
                rhs[k * B : (k + 1) * B, :] = feats[h][panel, col_ref[k, t] % R]
            for b in range(R):
                rows = slice(b * B, (b + 1) * B)
                acc[rows, :] += jnp.dot(
                    lhs[t, rows, :], rhs[...], preferred_element_type=F32
                )
            return 0

        lax.fori_loop(0, S, step, 0)

    rq = [slots(R), slots(R)]
    own_rows = pl.ds(pl.multiple_of(r * B, B), B)

    def f_finish(h):
        qs = fq[h][3]
        for d in range(X):
            arrived(feats[h].at[2 * ((x - d + X) % X) + 1 - c], qs + d)
        forward_products(h)
        for d in range(1, R):
            rd = (r + d) % R
            accb[h, d] = acc[pl.ds(pl.multiple_of(rd * B, B), B), :].astype(BF16)
            dev = at(y, zh * R + rd, x, c)
            copy(accb.at[h, d], rsin.at[h, d], rq[h] + d, dev, rq[h]).start()
        rsown[h] = acc[own_rows, :]

    def f_sent(h):
        qz, qy, qx, qs = fq[h]
        panel = feats[h].at[0]
        left(zbuf.at[h, pl.ds(0, Z - 1)], qz)
        for half in range(2):

            @pl.when(f_to(half) != y)
            def _():
                left(panel, qy + half)

        for d in range(X):
            left(panel, qs + d)
        for d in range(1, X):
            left(panel, qx + d * R)
        left(accb.at[h, pl.ds(1, R - 1)], rq[h])

    events = []
    top = len(levels)
    for h in range(2):
        for n in range(top):
            late = n + LATE * h
            events += [(late, 0, "gather", h, n), (late + 1, 1, "x", h, n)]
            events += [(late + 2, 2, "core", h, n)]
        events += [(top + 1.1 + LATE * h, 3, "finish", h, 0)]
    events += [(2.5, 4, "tiles", 0, 0)]
    for _, _, what, h, n in sorted(events):
        if what == "gather":
            for e in levels[n]:
                f_gather(h, e)
            for e in levels[n]:
                f_y(h, e)
        elif what == "x":
            for e in levels[n]:
                f_x(h, e)
        elif what == "core":
            for e in levels[n]:
                f_core(h, e)
        elif what == "tiles":
            for cp in loads[2:]:
                cp.wait()
            masked_tiles(row_ref, False)
        else:
            f_finish(h)
    for h in range(2):
        total = rsown[h]
        for d in range(1, R):
            arrived(rsin.at[h, d], rq[h] + d)
            total = total + rsin[h, d].astype(F32)
        agg_ref[:, h * HF : (h + 1) * HF] = total.astype(BF16)

    agg = agg_ref[...]
    preact = jnp.dot(agg, weight_ref[...], preferred_element_type=F32)
    sig = 1.0 / (1.0 + jnp.exp(-preact))
    slope = (cot_ref[...].astype(F32) * (sig * (1.0 + preact * (1.0 - sig)))).astype(BF16)
    back = lax.dot_general(
        slope, weight_ref[...], (((1,), (1,)), ((), ())), preferred_element_type=F32
    )
    gq = [slots(R), slots(R)]
    for h in range(2):
        gpanel[h][r] = back[:, h * HF : (h + 1) * HF].astype(BF16)
        for d in range(1, R):
            rd = (r + d) % R
            mine = gpanel[h].at[r]
            copy(mine, mine, gq[h] + d, at(y, zh * R + rd, x, c), gq[h]).start()
    act_ref[...] = (preact * sig).astype(BF16)
    w_own[...] = lax.dot_general(
        agg, slope, (((0,), (0,)), ((), ())), preferred_element_type=F32
    )
    half_rows = w_half.shape[0]
    x_rows = w_quart.shape[0]
    y_rows = w_eight.shape[0]

    def w_rows(i, n):
        return pl.ds(pl.multiple_of(i * n, n), n)

    qw = slots(1)
    go(copy(w_own.at[w_rows(1 - c, half_rows)], w_sib, qw, sib))
    masked_tiles(col_ref, True)
    for h in range(2):
        f_sent(h)
    arrived(w_sib, qw)
    w_half[...] = w_own[w_rows(c, half_rows), :] + w_sib[...]
    qw = slots(X)
    for d in range(1, X):
        xd = (x + d) % X
        go(copy(w_half.at[w_rows(xd, x_rows)], w_xin.at[x], qw + d, x_dev(d)))
    w_xin[x] = w_half[w_rows(x, x_rows), :]

    bq = [(slots(X), slots(X * R), slots(Z), slots(Z)) for _ in range(2)]

    def backward_products(h):
        for d in range(1, R):
            arrived(gpanel[h].at[(r - d + R) % R], gq[h] + d)

        def step(t, _):
            panel = (s - t + S) % S
            for k in range(K):
                rhs[k * B : (k + 1) * B, :] = gpanel[h][row_ref[k, t] % R]
            for b in range(R):
                rows = slice(b * B, (b + 1) * B)
                cbuf[h, panel, b] = jnp.dot(
                    lhs[t, rows, :], rhs[...], preferred_element_type=F32
                ).astype(BF16)

            @pl.when(panel % 2 != c)
            def _():
                d = (panel // 2 - x + X) % X
                copy(cbuf.at[h, panel], sibin.at[h, d], bq[h][0] + d, sib).start()

            return 0

        lax.fori_loop(0, S, step, 0)

    def b_x(h, e):
        w, b = role_of(e), slot_of(e) % R
        for d in range(1, X):
            xd = (x + d) % X

            @pl.when((xd < x) == (w == 0))
            def _():
                xout[h, d, b] = (
                    cbuf[h, 2 * xd + c, b].astype(F32) + sibin[h, d, b].astype(F32)
                ).astype(BF16)
                i = bq[h][1] + d * R
                copy(xout.at[h, d, b], xin.at[h, d, b], i + b, x_dev(d), i).start()

    def b_to(half):
        return ((2 * y + zh - r - (zh + r + half) % 2 + 2 * R) % R) // 2

    def b_y_to(e):
        return b_to(slot_of(e) // R)

    def b_y(h, e):
        w, b, i = role_of(e), slot_of(e) % R, bq[h][2] + number[e]
        own = cbuf[h, s, b].astype(F32)
        other = sibin[h, 0, b].astype(F32)
        ysum[...] = jnp.where(w == 0, own, 0.0) + jnp.where(w == c, other, 0.0)
        for d in range(1, X):

            @pl.when(((x - d + X) % X > x) == (w == 0))
            def _():
                arrived(xin.at[h, d, b], bq[h][1] + d * R + b)
                ysum[...] += xin[h, d, b].astype(F32)

        src = yout.at[h, number[e]]
        src[...] = ysum[...].astype(BF16)
        dst, to = zpart.at[h, slot_of(e)], b_y_to(e)

        @pl.when(to == y)
        def _():
            pltpu.make_async_copy(src, dst, recv.at[i]).start()

        @pl.when(to != y)
        def _():
            copy(src, dst, i, at(to, z, x, c), bq[h][2] + slot_of(e) // R).start()

    def b_z(h, e):
        g, m = e
        slot, n, qz = slot_of(e), number[e], bq[h][3]
        arrived(zpart.at[h, slot], bq[h][2] + n)
        val = zpart[h, slot].astype(F32)
        for k in children(e):
            arrived(zin.at[h, number[k]], qz + number[k])
            val = val + zin[h, number[k]].astype(F32)
        if m == 0:
            fgrad_ref[:, h * HF : (h + 1) * HF] = val.astype(BF16)
        else:
            zout[h, n] = val.astype(BF16)
            dev = z_dev(-g * (2 - m % 2))
            copy(zout.at[h, n], zin.at[h, n], qz + n, dev, qz).start()

    def w_piece(c_, x_, y_):
        at_row = c_ * half_rows + x_ * x_rows
        if y_ is None:
            return w_full.at[pl.ds(pl.multiple_of(at_row, x_rows), x_rows)]
        at_row = at_row + y_ * y_rows
        return w_full.at[pl.ds(pl.multiple_of(at_row, y_rows), y_rows)]

    def w_1():
        for d in range(1, X):
            arrived(w_xin.at[(x - d + X) % X], qw + d)
        w_quart[...] = functools.reduce(lambda a, b: a + b, [w_xin[i] for i in range(X)])
        i = slots(Y)
        for d in range(1, Y):
            yd = (y + d) % Y
            go(copy(w_quart.at[w_rows(yd, y_rows)], w_yin.at[y], i + d, y_dev(d)))
        w_yin[y] = w_quart[w_rows(y, y_rows), :]
        return i

    def w_2(i):
        for d in range(1, Y):
            arrived(w_yin.at[(y - d + Y) % Y], i + d)
        w_eight[...] = functools.reduce(lambda a, b: a + b, [w_yin[i] for i in range(Y)])
        w_zin[z] = w_eight[...]
        i = slots(Z)
        for d in range(1, Z):
            go(copy(w_eight, w_zin.at[z], i + d, z_dev(d)))
        return i

    def w_3(i):
        for d in range(1, Z):
            arrived(w_zin.at[(z - d + Z) % Z], i + d)
        piece = w_piece(c, x, y)
        piece[...] = functools.reduce(
            lambda a, b: a + b, [w_zin[i] for i in range(Z)]
        ) * (1.0 / math.sqrt(nodes))
        i = slots(Y)
        for d in range(1, Y):
            go(copy(piece, piece, i + d, y_dev(d)))
        return i

    def w_4(i):
        for d in range(1, Y):
            arrived(w_piece(c, x, (y - d + Y) % Y), i + d)
        piece = w_piece(c, x, None)
        i = slots(X)
        for d in range(1, X):
            go(copy(piece, piece, i + d, x_dev(d)))
        return i

    def w_5(i):
        for d in range(1, X):
            arrived(w_piece(c, (x - d + X) % X, None), i + d)
        rows = w_full.at[w_rows(c, half_rows)]
        i = slots(1)
        go(copy(rows, rows, i, sib))
        return i

    back_levels = levels[::-1]
    for h in range(2):
        backward_products(h)
        if h == 0:
            w_state = w_1()
        for d in range(X):
            arrived(sibin.at[h, d], bq[h][0] + d)
        for level in back_levels:
            for e in level:
                b_x(h, e)
    events = []
    for h in range(2):
        for n in range(top):
            late = n + BLATE * h
            events += [(late, 0, "y", h, n), (late + 2, 1, "z", h, n)]
    w_rest = [w_2, w_3, w_4, w_5]
    events += [(1.5 + n * 1.5, 2, "w", 0, n) for n in range(len(w_rest))]
    for _, _, what, h, n in sorted(events):
        if what == "w":
            w_state = w_rest[n](w_state)
        else:
            for e in back_levels[n]:
                (b_y if what == "y" else b_z)(h, e)
    arrived(w_full.at[w_rows(1 - c, half_rows)], w_state)
    wgrad_ref[...] = w_full[...]

    for h in range(2):
        qs, qx, qy, qz = bq[h]
        panel = cbuf.at[h, 0]
        left(accb.at[h, pl.ds(1, R - 1)], gq[h])
        for d in range(X):
            left(panel, qs + d)
        for d in range(1, X):
            left(panel, qx + d * R)
        for half in range(2):

            @pl.when(b_to(half) != y)
            def _():
                left(panel, qy + half)

        left(zout.at[h, pl.ds(0, Z - 1)], qz)
    for cp in sent:
        cp.wait_send()


def result_kernel(*refs):
    half = len(refs) // 2
    for src, dst in zip(refs[:half], refs[half:]):
        dst[...] = src[...]


def on_device(features, weight, cotangent, tile_row, tile_col, tile_count, tile_vals):
    B, F = features.shape
    R = lax.axis_size("rep")
    S = lax.axis_size("blk") // R
    K = tile_vals.shape[3]
    X, Y, Z = S // 2, R // 2, 2 * R
    nodes = B * R * R * S
    HF = F // 2
    dims = (R, X, Y, Z, S, K, B, HF, nodes)
    block = (B, F)
    part = (B, HF)
    vmem = pltpu.VMEM
    sems = 9 * Z + 4 * X * R + 8 * X + 4 * R + 2 * Y + 8
    scratch = [
        vmem((2, Z) + part, BF16),
        vmem((S + 1, R) + part, BF16),
        vmem((S + 1, R) + part, BF16),
        vmem((S, R * B, K * B), BF16),
        vmem((K * B, HF), BF16),
        vmem((R * B, HF), F32),
        vmem((2, R) + part, BF16),
        vmem((2, R) + part, BF16),
        vmem((2,) + part, F32),
        vmem(block, BF16),
        vmem((R,) + part, BF16),
        vmem((R,) + part, BF16),
        vmem((2, S, R) + part, BF16),
        vmem((2, X, R) + part, BF16),
        vmem((2, X, R) + part, BF16),
        vmem((2, X, R) + part, BF16),
        vmem((2, Z) + part, BF16),
        vmem((2, Z) + part, BF16),
        vmem((2, Z) + part, BF16),
        vmem((2, Z) + part, BF16),
        vmem((F, F), F32),
        vmem((F, F), F32),
        vmem((F // 2, F), F32),
        vmem((F // 2, F), F32),
        vmem((X, F // 2 // X, F), F32),
        vmem((F // 2 // X, F), F32),
        vmem((Y, F // 2 // X // Y, F), F32),
        vmem((F // 2 // X // Y, F), F32),
        vmem((Z, F // 2 // X // Y, F), F32),
        vmem((F, F), BF16),
        vmem(block, BF16),
        pltpu.SMEM((K, S), jnp.int32),
        pltpu.SMEM((K, S), jnp.int32),
        pltpu.SMEM((S,), jnp.int32),
        vmem((S * K, B, B), BF16),
        vmem(part, F32),
        pltpu.SemaphoreType.DMA((sems,)),
        pltpu.SemaphoreType.DMA((sems,)),
        pltpu.SemaphoreType.DMA((8,)),
    ]
    in_vmem = pl.BlockSpec(memory_space=pltpu.VMEM)
    in_hbm = pl.BlockSpec(memory_space=pltpu.HBM)
    results = pl.pallas_call(
        functools.partial(layer_kernel, dims),
        out_shape=(
            jax.ShapeDtypeStruct(block, BF16),
            jax.ShapeDtypeStruct((F, F), F32),
            jax.ShapeDtypeStruct(block, BF16),
        ),
        in_specs=[in_hbm] * 7,
        out_specs=(in_vmem, in_vmem, in_vmem),
        scratch_shapes=scratch,
        compiler_params=pltpu.CompilerParams(
            collective_id=0, has_side_effects=True, vmem_limit_bytes=63 << 20
        ),
        name="layer",
    )(
        features,
        weight,
        cotangent,
        tile_row[0, 0].T,
        tile_col[0, 0].T,
        tile_count[0, 0],
        tile_vals.reshape((S * K, B, B)),
    )
    if not TAIL:
        return results
    return pl.pallas_call(
        result_kernel,
        out_shape=tuple(jax.ShapeDtypeStruct(v.shape, v.dtype) for v in results),
        in_specs=[in_vmem] * 3,
        out_specs=(in_vmem,) * 3,
        name="results",
    )(*results)


def solution(mesh):
    return jax.shard_map(
        on_device,
        mesh=mesh,
        in_specs=(
            P(("rep", "blk"), None),
            P(),
            P(("rep", "blk"), None),
            P("rep", "blk", None, None),
            P("rep", "blk", None, None),
            P("rep", "blk", None),
            P("rep", "blk", None, None, None, None),
        ),
        out_specs=(P(("rep", "blk"), None), P(), P(("rep", "blk"), None)),
        check_vma=False,
    )
```

```python
import functools
import math

import jax
import jax.numpy as jnp
from jax import lax
from jax.experimental import pallas as pl
from jax.experimental.pallas import tpu as pltpu
from jax.sharding import PartitionSpec as P

BF16 = jnp.bfloat16
LATE = 2.5
BLATE = 2.5
TAIL = True
F32 = jnp.float32
MESH = pl.DeviceIdType.MESH


def layer_kernel(
    dims,
    feat_hbm,
    weight_hbm,
    cot_hbm,
    row_hbm,
    col_hbm,
    count_hbm,
    tile_hbm,
    act_ref,
    wgrad_ref,
    fgrad_ref,
    zbuf,
    feats_0,
    feats_1,
    lhs,
    rhs,
    acc,
    accb,
    rsin,
    rsown,
    agg_ref,
    gpanel_0,
    gpanel_1,
    cbuf,
    sibin,
    xout,
    xin,
    yout,
    zpart,
    zin,
    zout,
    w_own,
    w_full,
    w_sib,
    w_half,
    w_xin,
    w_quart,
    w_yin,
    w_eight,
    w_zin,
    weight_ref,
    cot_ref,
    row_ref,
    col_ref,
    count_ref,
    tile_ref,
    ysum,
    send,
    recv,
    load,
):
    R, X, Y, Z, S, K, B, HF, nodes = dims
    feats, gpanel = (feats_0, feats_1), (gpanel_0, gpanel_1)
    r = lax.axis_index("rep")
    p = lax.axis_index("blk")
    c = p % 2
    x = (p // 2) % X
    zh = (p // S) % 2
    y = p // (2 * S)
    s = p % S
    z = zh * R + r

    def at(y_, z_, x_, c_):
        return {"rep": z_ % R, "blk": ((y_ * 2 + z_ // R) * X + x_) * 2 + c_}

    def z_dev(off):
        return at(y, (z + off + Z) % Z, x, c)

    def y_dev(off):
        return at((y + off) % Y, z, x, c)

    def x_dev(off):
        return at(y, z, (x + off) % X, c)

    sib = at(y, z, x, 1 - c)
    used = [0]

    def slots(n):
        used[0] += n
        return used[0] - n

    def copy(src, dst, i, dev, out=None):
        return pltpu.make_async_remote_copy(
            src_ref=src,
            dst_ref=dst,
            send_sem=send.at[i if out is None else out],
            recv_sem=recv.at[i],
            device_id=dev,
            device_id_type=MESH,
        )

    def left(like, i):
        copy(like, like, i, sib).wait_send()

    def arrived(dst, i):
        copy(dst, dst, i, sib).wait_recv()

    def half_cols(h):
        return pl.ds(h * HF, HF)

    loads = [
        pltpu.make_async_copy(src, dst, load.at[i])
        for i, (src, dst) in enumerate(
            [
                (feat_hbm.at[:, half_cols(0)], zbuf.at[0, z]),
                (feat_hbm.at[:, half_cols(1)], zbuf.at[1, z]),
                (row_hbm, row_ref),
                (col_hbm, col_ref),
                (count_hbm, count_ref),
                (tile_hbm, tile_ref),
                (weight_hbm, weight_ref),
                (cot_hbm, cot_ref),
            ]
        )
    ]
    for cp in loads:
        cp.start()

    near = sorted({d % Z for d in (1, 2, -1, -2)} - {0})
    peers = [z_dev(d) for d in near] + [y_dev(d) for d in range(1, Y)]
    peers += [x_dev(d) for d in range(1, X)] + [sib]
    barrier = pltpu.get_barrier_semaphore()
    for dev in peers:
        pl.semaphore_signal(barrier, inc=1, device_id=dev, device_id_type=MESH)
    loads[0].wait()
    loads[1].wait()
    pl.semaphore_wait(barrier, len(peers))

    sent = []

    def go(cp):
        cp.start()
        sent.append(cp)

    up, down = Z // 2, Z - 1 - Z // 2
    levels = [[(1, 0)]]
    for top in range(2, up + 2, 2):
        level = [(g, m) for m in (top, top - 1) for g in (1, -1)]
        levels.append([(g, m) for g, m in level if m <= (up if g > 0 else down)])
    order = [e for level in levels for e in level]
    number = {e: n for n, e in enumerate(order)}

    def slot_of(e):
        return (z - e[0] * e[1] + Z) % Z

    def children(e):
        g, m = e
        if m % 2:
            return []
        both = [(1, 1), (-1, 1), (1, 2), (-1, 2)] if m == 0 else [(g, m + 1), (g, m + 2)]
        return [k for k in both if k in number]

    def role_of(e):
        return (zh + r + slot_of(e) // R) % 2

    fq = [(slots(Z), slots(Z), slots(X * R), slots(X)) for _ in range(2)]

    def f_gather(h, e):
        slot, qz = slot_of(e), fq[h][0]
        block = zbuf.at[h, slot]
        if e[1]:
            arrived(block, qz + number[e])
        for k in children(e)[::-1]:
            hop = k[0] * (k[1] - e[1])
            copy(block, block, qz + number[k], z_dev(hop), qz).start()

    def f_to(half):
        return ((2 * y + half + (zh + r + half) % 2 + r - zh + R) % R) // 2

    def f_y_to(e):
        return f_to(slot_of(e) // R)

    def f_y_block(h, e):
        w = role_of(e)
        return feats[h].at[s * (1 - w) + S * w, slot_of(e) % R]

    def f_y(h, e):
        slot, to, i = slot_of(e), f_y_to(e), fq[h][1] + number[e]

        @pl.when(to == y)
        def _():
            pltpu.make_async_copy(
                zbuf.at[h, slot], f_y_block(h, e), recv.at[i]
            ).start()

        @pl.when(to != y)
        def _():
            out = fq[h][1] + slot // R
            copy(zbuf.at[h, slot], f_y_block(h, e), i, at(to, z, x, c), out).start()

    def f_x(h, e):
        w, b = role_of(e), slot_of(e) % R
        src = f_y_block(h, e)
        _, qy, qx, qs = fq[h]
        arrived(src, qy + number[e])
        for d in range(1, X):

            @pl.when((x < (x + d) % X) == (w == 0))
            def _():
                i = qx + d * R
                copy(src, feats[h].at[s, b], i + b, x_dev(d), i).start()

        @pl.when(w == c)
        def _():
            copy(src, feats[h].at[s, b], qs, sib).start()

    def f_core(h, e):
        w, b = role_of(e), slot_of(e) % R
        _, _, qx, qs = fq[h]
        for d in range(1, X):
            xs = (x - d + X) % X

            @pl.when((xs < x) == (w == 0))
            def _():
                block = feats[h].at[2 * xs + c, b]
                arrived(block, qx + d * R + b)
                copy(block, block, qs + d, sib).start()

    def masked_tiles(ids, turned):
        def step(t, _):
            for k in range(K):
                live = k < count_ref[t]
                block = ids[k, t] % R
                tile = tile_ref[t * K + k]
                if turned:
                    tile = tile.T
                for b in range(R):
                    keep = jnp.logical_and(live, block == b)
                    lhs[t, b * B : (b + 1) * B, k * B : (k + 1) * B] = jnp.where(
                        keep, tile, jnp.zeros_like(tile)
                    )
            return 0

        lax.fori_loop(0, S, step, 0)

    def forward_products(h):
        acc[...] = jnp.zeros_like(acc)

        def step(t, _):
            panel = (s - t + S) % S
            for k in range(K):
                rhs[k * B : (k + 1) * B, :] = feats[h][panel, col_ref[k, t] % R]
            for b in range(R):
                rows = slice(b * B, (b + 1) * B)
                acc[rows, :] += jnp.dot(
                    lhs[t, rows, :], rhs[...], preferred_element_type=F32
                )
            return 0

        lax.fori_loop(0, S, step, 0)

    rq = [slots(R), slots(R)]
    near_first = sorted(range(1, R), key=lambda d: min(d, R - d))
    own_rows = pl.ds(pl.multiple_of(r * B, B), B)

    def f_finish(h):
        qs = fq[h][3]
        for d in range(X):
            arrived(feats[h].at[2 * ((x - d + X) % X) + 1 - c], qs + d)
        forward_products(h)
        for d in near_first:
            rd = (r + d) % R
            accb[h, d] = acc[pl.ds(pl.multiple_of(rd * B, B), B), :].astype(BF16)
            dev = at(y, zh * R + rd, x, c)
            copy(accb.at[h, d], rsin.at[h, d], rq[h] + d, dev, rq[h]).start()
        rsown[h] = acc[own_rows, :]

    def f_sent(h):
        qz, qy, qx, qs = fq[h]
        panel = feats[h].at[0]
        left(zbuf.at[h, pl.ds(0, Z - 1)], qz)
        for half in range(2):

            @pl.when(f_to(half) != y)
            def _():
                left(panel, qy + half)

        for d in range(X):
            left(panel, qs + d)
        for d in range(1, X):
            left(panel, qx + d * R)
        left(accb.at[h, pl.ds(1, R - 1)], rq[h])

    events = []
    top = len(levels)
    for h in range(2):
        for n in range(top):
            late = n + LATE * h
            events += [(late, 0, "gather", h, n), (late + 1, 1, "x", h, n)]
            events += [(late + 2, 2, "core", h, n)]
        events += [(top + 1.1 + LATE * h, 3, "finish", h, 0)]
    events += [(2.5, 4, "tiles", 0, 0)]
    for _, _, what, h, n in sorted(events):
        if what == "gather":
            for e in levels[n]:
                f_gather(h, e)
            for e in levels[n]:
                f_y(h, e)
        elif what == "x":
            for e in levels[n]:
                f_x(h, e)
        elif what == "core":
            for e in levels[n]:
                f_core(h, e)
        elif what == "tiles":
            for cp in loads[2:]:
                cp.wait()
            masked_tiles(row_ref, False)
        else:
            f_finish(h)
    for h in range(2):
        total = rsown[h]
        for d in range(1, R):
            arrived(rsin.at[h, d], rq[h] + d)
            total = total + rsin[h, d].astype(F32)
        agg_ref[:, h * HF : (h + 1) * HF] = total.astype(BF16)

    agg = agg_ref[...]
    preact = jnp.dot(agg, weight_ref[...], preferred_element_type=F32)
    sig = 1.0 / (1.0 + jnp.exp(-preact))
    slope = (cot_ref[...].astype(F32) * (sig * (1.0 + preact * (1.0 - sig)))).astype(BF16)
    back = lax.dot_general(
        slope, weight_ref[...], (((1,), (1,)), ((), ())), preferred_element_type=F32
    )
    gq = [slots(R), slots(R)]
    for h in range(2):
        gpanel[h][r] = back[:, h * HF : (h + 1) * HF].astype(BF16)
        for d in near_first:
            rd = (r + d) % R
            mine = gpanel[h].at[r]
            copy(mine, mine, gq[h] + d, at(y, zh * R + rd, x, c), gq[h]).start()
    act_ref[...] = (preact * sig).astype(BF16)
    w_own[...] = lax.dot_general(
        agg, slope, (((0,), (0,)), ((), ())), preferred_element_type=F32
    )
    half_rows = w_half.shape[0]
    x_rows = w_quart.shape[0]
    y_rows = w_eight.shape[0]

    def w_rows(i, n):
        return pl.ds(pl.multiple_of(i * n, n), n)

    qw = slots(1)
    go(copy(w_own.at[w_rows(1 - c, half_rows)], w_sib, qw, sib))
    masked_tiles(col_ref, True)
    for h in range(2):
        f_sent(h)
    arrived(w_sib, qw)
    w_half[...] = w_own[w_rows(c, half_rows), :] + w_sib[...]
    qw = slots(X)
    for d in range(1, X):
        xd = (x + d) % X
        go(copy(w_half.at[w_rows(xd, x_rows)], w_xin.at[x], qw + d, x_dev(d)))
    w_xin[x] = w_half[w_rows(x, x_rows), :]

    bq = [(slots(X), slots(X * R), slots(Z), slots(Z)) for _ in range(2)]

    def backward_products(h):
        for d in range(1, R):
            arrived(gpanel[h].at[(r - d + R) % R], gq[h] + d)

        def step(t, _):
            panel = (s - t + S) % S
            for k in range(K):
                rhs[k * B : (k + 1) * B, :] = gpanel[h][row_ref[k, t] % R]
            for b in range(R):
                rows = slice(b * B, (b + 1) * B)
                cbuf[h, panel, b] = jnp.dot(
                    lhs[t, rows, :], rhs[...], preferred_element_type=F32
                ).astype(BF16)

            @pl.when(panel % 2 != c)
            def _():
                d = (panel // 2 - x + X) % X
                copy(cbuf.at[h, panel], sibin.at[h, d], bq[h][0] + d, sib).start()

            return 0

        lax.fori_loop(0, S, step, 0)

    def b_x(h, e):
        w, b = role_of(e), slot_of(e) % R
        for d in range(1, X):
            xd = (x + d) % X

            @pl.when((xd < x) == (w == 0))
            def _():
                xout[h, d, b] = (
                    cbuf[h, 2 * xd + c, b].astype(F32) + sibin[h, d, b].astype(F32)
                ).astype(BF16)
                i = bq[h][1] + d * R
                copy(xout.at[h, d, b], xin.at[h, d, b], i + b, x_dev(d), i).start()

    def b_to(half):
        return ((2 * y + zh - r - (zh + r + half) % 2 + 2 * R) % R) // 2

    def b_y_to(e):
        return b_to(slot_of(e) // R)

    def b_y(h, e):
        w, b, i = role_of(e), slot_of(e) % R, bq[h][2] + number[e]
        own = cbuf[h, s, b].astype(F32)
        other = sibin[h, 0, b].astype(F32)
        ysum[...] = jnp.where(w == 0, own, 0.0) + jnp.where(w == c, other, 0.0)
        for d in range(1, X):

            @pl.when(((x - d + X) % X > x) == (w == 0))
            def _():
                arrived(xin.at[h, d, b], bq[h][1] + d * R + b)
                ysum[...] += xin[h, d, b].astype(F32)

        src = yout.at[h, number[e]]
        src[...] = ysum[...].astype(BF16)
        dst, to = zpart.at[h, slot_of(e)], b_y_to(e)

        @pl.when(to == y)
        def _():
            pltpu.make_async_copy(src, dst, recv.at[i]).start()

        @pl.when(to != y)
        def _():
            copy(src, dst, i, at(to, z, x, c), bq[h][2] + slot_of(e) // R).start()

    def b_z(h, e):
        g, m = e
        slot, n, qz = slot_of(e), number[e], bq[h][3]
        arrived(zpart.at[h, slot], bq[h][2] + n)
        val = zpart[h, slot].astype(F32)
        for k in children(e):
            arrived(zin.at[h, number[k]], qz + number[k])
            val = val + zin[h, number[k]].astype(F32)
        if m == 0:
            fgrad_ref[:, h * HF : (h + 1) * HF] = val.astype(BF16)
        else:
            zout[h, n] = val.astype(BF16)
            dev = z_dev(-g * (2 - m % 2))
            copy(zout.at[h, n], zin.at[h, n], qz + n, dev, qz).start()

    def w_piece(c_, x_, y_):
        at_row = c_ * half_rows + x_ * x_rows
        if y_ is None:
            return w_full.at[pl.ds(pl.multiple_of(at_row, x_rows), x_rows)]
        at_row = at_row + y_ * y_rows
        return w_full.at[pl.ds(pl.multiple_of(at_row, y_rows), y_rows)]

    def w_1():
        for d in range(1, X):
            arrived(w_xin.at[(x - d + X) % X], qw + d)
        w_quart[...] = functools.reduce(lambda a, b: a + b, [w_xin[i] for i in range(X)])
        i = slots(Y)
        for d in range(1, Y):
            yd = (y + d) % Y
            go(copy(w_quart.at[w_rows(yd, y_rows)], w_yin.at[y], i + d, y_dev(d)))
        w_yin[y] = w_quart[w_rows(y, y_rows), :]
        return i

    def w_2(i):
        for d in range(1, Y):
            arrived(w_yin.at[(y - d + Y) % Y], i + d)
        w_eight[...] = functools.reduce(lambda a, b: a + b, [w_yin[i] for i in range(Y)])
        w_zin[z] = w_eight[...]
        i = slots(Z)
        for d in range(1, Z):
            go(copy(w_eight, w_zin.at[z], i + d, z_dev(d)))
        return i

    def w_3(i):
        for d in range(1, Z):
            arrived(w_zin.at[(z - d + Z) % Z], i + d)
        piece = w_piece(c, x, y)
        piece[...] = functools.reduce(
            lambda a, b: a + b, [w_zin[i] for i in range(Z)]
        ) * (1.0 / math.sqrt(nodes))
        i = slots(Y)
        for d in range(1, Y):
            go(copy(piece, piece, i + d, y_dev(d)))
        return i

    def w_4(i):
        for d in range(1, Y):
            arrived(w_piece(c, x, (y - d + Y) % Y), i + d)
        piece = w_piece(c, x, None)
        i = slots(X)
        for d in range(1, X):
            go(copy(piece, piece, i + d, x_dev(d)))
        return i

    def w_5(i):
        for d in range(1, X):
            arrived(w_piece(c, (x - d + X) % X, None), i + d)
        rows = w_full.at[w_rows(c, half_rows)]
        i = slots(1)
        go(copy(rows, rows, i, sib))
        return i

    back_levels = levels[::-1]
    for h in range(2):
        backward_products(h)
        if h == 0:
            w_state = w_1()
        for d in range(X):
            arrived(sibin.at[h, d], bq[h][0] + d)
        for level in back_levels:
            for e in level:
                b_x(h, e)
    events = []
    for h in range(2):
        for n in range(top):
            late = n + BLATE * h
            events += [(late, 0, "y", h, n), (late + 2, 1, "z", h, n)]
    w_rest = [w_2, w_3, w_4, w_5]
    events += [(1.5 + n * 1.5, 2, "w", 0, n) for n in range(len(w_rest))]
    for _, _, what, h, n in sorted(events):
        if what == "w":
            w_state = w_rest[n](w_state)
        else:
            for e in back_levels[n]:
                (b_y if what == "y" else b_z)(h, e)
    arrived(w_full.at[w_rows(1 - c, half_rows)], w_state)
    wgrad_ref[...] = w_full[...]

    for h in range(2):
        qs, qx, qy, qz = bq[h]
        panel = cbuf.at[h, 0]
        left(accb.at[h, pl.ds(1, R - 1)], gq[h])
        for d in range(X):
            left(panel, qs + d)
        for d in range(1, X):
            left(panel, qx + d * R)
        for half in range(2):

            @pl.when(b_to(half) != y)
            def _():
                left(panel, qy + half)

        left(zout.at[h, pl.ds(0, Z - 1)], qz)
    for cp in sent:
        cp.wait_send()


def result_kernel(*refs):
    half = len(refs) // 2
    for src, dst in zip(refs[:half], refs[half:]):
        dst[...] = src[...]


def on_device(features, weight, cotangent, tile_row, tile_col, tile_count, tile_vals):
    B, F = features.shape
    R = lax.axis_size("rep")
    S = lax.axis_size("blk") // R
    K = tile_vals.shape[3]
    X, Y, Z = S // 2, R // 2, 2 * R
    nodes = B * R * R * S
    HF = F // 2
    dims = (R, X, Y, Z, S, K, B, HF, nodes)
    block = (B, F)
    part = (B, HF)
    vmem = pltpu.VMEM
    sems = 9 * Z + 4 * X * R + 8 * X + 4 * R + 2 * Y + 8
    scratch = [
        vmem((2, Z) + part, BF16),
        vmem((S + 1, R) + part, BF16),
        vmem((S + 1, R) + part, BF16),
        vmem((S, R * B, K * B), BF16),
        vmem((K * B, HF), BF16),
        vmem((R * B, HF), F32),
        vmem((2, R) + part, BF16),
        vmem((2, R) + part, BF16),
        vmem((2,) + part, F32),
        vmem(block, BF16),
        vmem((R,) + part, BF16),
        vmem((R,) + part, BF16),
        vmem((2, S, R) + part, BF16),
        vmem((2, X, R) + part, BF16),
        vmem((2, X, R) + part, BF16),
        vmem((2, X, R) + part, BF16),
        vmem((2, Z) + part, BF16),
        vmem((2, Z) + part, BF16),
        vmem((2, Z) + part, BF16),
        vmem((2, Z) + part, BF16),
        vmem((F, F), F32),
        vmem((F, F), F32),
        vmem((F // 2, F), F32),
        vmem((F // 2, F), F32),
        vmem((X, F // 2 // X, F), F32),
        vmem((F // 2 // X, F), F32),
        vmem((Y, F // 2 // X // Y, F), F32),
        vmem((F // 2 // X // Y, F), F32),
        vmem((Z, F // 2 // X // Y, F), F32),
        vmem((F, F), BF16),
        vmem(block, BF16),
        pltpu.SMEM((K, S), jnp.int32),
        pltpu.SMEM((K, S), jnp.int32),
        pltpu.SMEM((S,), jnp.int32),
        vmem((S * K, B, B), BF16),
        vmem(part, F32),
        pltpu.SemaphoreType.DMA((sems,)),
        pltpu.SemaphoreType.DMA((sems,)),
        pltpu.SemaphoreType.DMA((8,)),
    ]
    in_vmem = pl.BlockSpec(memory_space=pltpu.VMEM)
    in_hbm = pl.BlockSpec(memory_space=pltpu.HBM)
    results = pl.pallas_call(
        functools.partial(layer_kernel, dims),
        out_shape=(
            jax.ShapeDtypeStruct(block, BF16),
            jax.ShapeDtypeStruct((F, F), F32),
            jax.ShapeDtypeStruct(block, BF16),
        ),
        in_specs=[in_hbm] * 7,
        out_specs=(in_vmem, in_vmem, in_vmem),
        scratch_shapes=scratch,
        compiler_params=pltpu.CompilerParams(
            collective_id=0, has_side_effects=True, vmem_limit_bytes=63 << 20
        ),
        name="layer",
    )(
        features,
        weight,
        cotangent,
        tile_row[0, 0].T,
        tile_col[0, 0].T,
        tile_count[0, 0],
        tile_vals.reshape((S * K, B, B)),
    )
    if not TAIL:
        return results
    return pl.pallas_call(
        result_kernel,
        out_shape=tuple(jax.ShapeDtypeStruct(v.shape, v.dtype) for v in results),
        in_specs=[in_vmem] * 3,
        out_specs=(in_vmem,) * 3,
        name="results",
    )(*results)


def solution(mesh):
    return jax.shard_map(
        on_device,
        mesh=mesh,
        in_specs=(
            P(("rep", "blk"), None),
            P(),
            P(("rep", "blk"), None),
            P("rep", "blk", None, None),
            P("rep", "blk", None, None),
            P("rep", "blk", None),
            P("rep", "blk", None, None, None, None),
        ),
        out_specs=(P(("rep", "blk"), None), P(), P(("rep", "blk"), None)),
        check_vma=False,
    )
```
